128 devices in a mesh: ctx: 32 (over y, x, core), dp: 4 (over z).
Axes of the slice: x: 4, y: 4, z: 4, core: 2. Of those that a mesh axis runs over, the one named last changes fastest.
Arguments:
- query: bfloat16 [4, 6144, 4096], P('dp', 'ctx'), may hold values from -6 to 6
- key_value: bfloat16 [4, 6144, 1024], P('dp', 'ctx'), may hold values from -6 to 6
- upstream: bfloat16 [4, 6144, 4096], P('dp', 'ctx'), may hold values from -6 to 6
- log_ratio: float32 [4, 6144], P('dp', 'ctx'), may hold values from -4 to 1
- doc_starts: int32 [4, 64], P('dp'), may hold values from 0 to 6144, as said below
- answer_counts: int32 [4, 64], P('dp'), may hold values from 0 to 768, as said below
Outputs:
- d_query: bfloat16 [4, 6144, 4096], P('dp', 'ctx')
- d_key_value: bfloat16 [4, 6144, 1024], P('dp', 'ctx')
The draws below stay inside these ranges and needn't reach their ends.
Inputs may be any that keep to these rules, and one draw needn't show every extreme that they name: `doc_starts`: used slots come first; each sequence's documents start at the listed positions in rising order, the first at 0, together covering all 6144 positions; unused slots hold 6144; every document has 96 to 768 positions, and every sequence has a document of exactly 768 positions. A document's answer positions are its last answer_counts positions; a used slot holds half of the document's length (rounded down) up to all of it, an unused slot 0; every sequence has a document of 768 positions that are all answer positions.
All inputs are finite; a program needn't handle non-finite values.
Results may differ from the reference program's by a relative error of at most 0.011.
Values may be sent and summed in bfloat16 or wider, within the bound.
No kernel may reach another device: no remote copies, remote signals or barrier semaphores. Data moves between devices by JAX's collectives and lax.ppermute only.
A program may use at most 64 MiB of HBM per device.

```python
import jax
import jax.numpy as jnp
from jax import lax

HQ = 32
HK = 4
DH = 128
TOK_DEV = 192
SPAN = 4
LOSS_SCALE = 65536
NSEQ = 4
SEQ = 6144
DOC_MOST = 768
DOC_LEAST = 96
MAXDOC = 64


def doc_layout(key):
    base_key = jax.random.fold_in(key, 11)
    slot_index = jnp.arange(MAXDOC, dtype=jnp.int32)
    fit_count = (SEQ - DOC_LEAST - DOC_MOST) // (DOC_MOST - DOC_LEAST) + 1

    def one_sequence(seq_key):
        length_key, long_key, share_key = jax.random.split(seq_key, 3)
        lengths = jax.random.randint(length_key, (MAXDOC,), DOC_LEAST, DOC_MOST - DOC_LEAST + 1, dtype=jnp.int32)
        longest = jax.random.randint(long_key, (), 0, fit_count, dtype=jnp.int32)
        lengths = jnp.where(slot_index == longest, DOC_MOST, lengths)
        ends_at = jnp.cumsum(lengths)
        starts = ends_at - lengths
        used = starts <= SEQ - DOC_LEAST
        next_used = jnp.concatenate([used[1:], jnp.zeros((1,), jnp.bool_)])
        true_len = jnp.where(next_used, lengths, SEQ - starts)
        shares = jax.random.randint(share_key, (MAXDOC,), 0, 65536, dtype=jnp.int32)
        halves = true_len // 2
        counts = halves + shares * (true_len - halves + 1) // 65536
        counts = jnp.where(slot_index == longest, true_len, counts)
        return (jnp.where(used, starts, SEQ), jnp.where(used, counts, 0))
    return jax.vmap(one_sequence)(jax.random.split(base_key, NSEQ))


def draw_doc_starts(key, part):
    return doc_layout(key)[0].astype(jnp.int32)


def draw_answer_counts(key, part):
    return doc_layout(key)[1].astype(jnp.int32)


def draw_query(key, part):
    result_rows = jnp.clip(jax.random.normal(jax.random.fold_in(key, 31), (NSEQ, SEQ, HQ, DH)), -6.0, 6.0)
    return result_rows.reshape(NSEQ, SEQ, HQ * DH).astype(jnp.bfloat16)


def draw_key_value(key, part):
    stacked = jnp.clip(jax.random.normal(jax.random.fold_in(key, 32), (NSEQ, SEQ, 2, HK, DH)), -6.0, 6.0)
    return stacked.reshape(NSEQ, SEQ, 2 * HK * DH).astype(jnp.bfloat16)


def steps_of(own_key, dims, pieces, smallest, largest):
    def one(dim, parts):
        steps = jax.random.uniform(jax.random.fold_in(jax.random.fold_in(own_key, 6), dim), (parts,), jnp.float32, smallest / len(pieces), largest / len(pieces))
        return jnp.repeat(jnp.exp(steps), dims[dim] // parts).reshape((-1,) + (1,) * (len(dims) - dim - 1))

    level = one(*pieces[0])
    for cut in pieces[1:]:
        level = level * one(*cut)
    return level


def scatter_about(rng, dims, width, limit, cuts=(), held_as=jnp.bfloat16):
    values = width * jax.random.normal(rng, dims, jnp.float32)
    if cuts:
        values = values * steps_of(rng, dims, cuts, -0.22, 0.18)
    return jnp.clip(values, -limit, limit).astype(held_as)


def setup_inputs(seed: int = 0) -> dict:
    keys = jax.random.split(jax.random.key(seed), 7)
    query = draw_query(jax.random.fold_in(keys[6], 71), 0)
    key_value = draw_key_value(jax.random.fold_in(keys[6], 71), 0)
    upstream = scatter_about(keys[2], (NSEQ, SEQ, HQ * DH), 1.0, 6.0, ((0, 4), (1, 32)))
    log_ratio = jnp.clip(-4.0 + 5.0 * jax.random.uniform(keys[3], (NSEQ, SEQ), jnp.float32) ** steps_of(keys[3], (NSEQ, SEQ), ((0, 4), (1, 32)), -0.2, 0.2), -4.0, 1.0)
    doc_starts = draw_doc_starts(jax.random.fold_in(keys[6], 71), 0)
    answer_counts = draw_answer_counts(jax.random.fold_in(keys[6], 71), 0)
    return {"query": query, "key_value": key_value, "upstream": upstream, "log_ratio": log_ratio, "doc_starts": doc_starts, "answer_counts": answer_counts}


def doc_index(starts, positions):
    return jnp.sum((starts[None, :] <= positions[:, None]).astype(jnp.int32), axis=1) - 1


def head_block(query_head, out_grad, key_head, value_head, visible):
    score_scale = DH ** -0.5
    query_wide = query_head.astype(jnp.float32)
    grad_wide = out_grad.astype(jnp.float32)
    key_wide = key_head.astype(jnp.float32)
    value_wide = value_head.astype(jnp.float32)
    scores = jnp.einsum("tgd,kd->gtk", query_wide, key_wide) * score_scale
    scores = jnp.where(visible[None], scores, -1e30)
    row_max = jnp.max(scores, axis=2, keepdims=True)
    row_total = jnp.sum(jnp.exp(scores - row_max), axis=2, keepdims=True)
    prob_full = jnp.exp(scores - (row_max + jnp.log(row_total)))
    prob_low = prob_full.astype(jnp.bfloat16)
    prob_back = prob_low.astype(jnp.float32)
    attended = jnp.einsum("gtk,kd->tgd", prob_back, value_wide)
    row_delta = jnp.sum(grad_wide * attended, axis=2)
    d_probs = jnp.einsum("tgd,kd->gtk", grad_wide, value_wide)
    d_scores = (prob_full * (d_probs - jnp.transpose(row_delta)[:, :, None])).astype(jnp.bfloat16)
    score_back = d_scores.astype(jnp.float32)
    query_grad = jnp.einsum("gtk,kd->tgd", score_back, key_wide) * score_scale
    key_grad = jnp.einsum("gtk,tgd->kd", score_back, query_wide) * score_scale
    value_grad = jnp.einsum("gtk,tgd->kd", prob_back, grad_wide)
    return query_grad, key_grad, value_grad


def sequence_grads(query, key_value, out_grad, doc_of):
    seq_len = query.shape[0]
    kv_width = key_value.shape[1]
    reach = SPAN * TOK_DEV
    window = reach + TOK_DEV
    group_size = HQ // HK
    padded_kv = jnp.concatenate([jnp.zeros((reach, kv_width), key_value.dtype), key_value], axis=0)
    padded_doc = jnp.concatenate([jnp.full((reach,), -1, jnp.int32), doc_of.astype(jnp.int32)], axis=0)

    def step(accum, block):
        first = (block * TOK_DEV).astype(jnp.int32)
        query_rows = lax.dynamic_slice_in_dim(query, first, TOK_DEV, 0)
        grad_rows = lax.dynamic_slice_in_dim(out_grad, first, TOK_DEV, 0)
        doc_rows = lax.dynamic_slice_in_dim(doc_of.astype(jnp.int32), first, TOK_DEV, 0)
        keys_all = lax.dynamic_slice_in_dim(padded_kv, first, window, 0)
        doc_keys = lax.dynamic_slice_in_dim(padded_doc, first, window, 0)
        query_pos = first + jnp.arange(TOK_DEV, dtype=jnp.int32)
        key_pos = first - reach + jnp.arange(window, dtype=jnp.int32)
        visible = (doc_rows[:, None] == doc_keys[None, :]) & (key_pos[None, :] <= query_pos[:, None])
        query_parts = []
        key_parts = []
        value_parts = []
        for head_group in range(HK):
            lo_col = head_group * group_size * DH
            hi_col = lo_col + group_size * DH
            query_head = query_rows[:, lo_col:hi_col].reshape(TOK_DEV, group_size, DH)
            grad_head = grad_rows[:, lo_col:hi_col].reshape(TOK_DEV, group_size, DH)
            key_head = keys_all[:, head_group * DH:(head_group + 1) * DH]
            value_head = keys_all[:, HK * DH + head_group * DH:HK * DH + (head_group + 1) * DH]
            query_grad, key_grad, value_grad = head_block(query_head, grad_head, key_head, value_head, visible)
            query_parts.append(query_grad.reshape(TOK_DEV, group_size * DH))
            key_parts.append(key_grad)
            value_parts.append(value_grad)
        block_grad = jnp.concatenate(key_parts + value_parts, axis=1)
        current = lax.dynamic_slice_in_dim(accum, first, window, 0)
        accum = lax.dynamic_update_slice_in_dim(accum, current + block_grad, first, 0)
        return accum, jnp.concatenate(query_parts, axis=1).astype(jnp.bfloat16)

    start_accum = jnp.zeros((seq_len + reach, kv_width), jnp.float32)
    accum, query_blocks = lax.scan(step, start_accum, jnp.arange(seq_len // TOK_DEV, dtype=jnp.int32))
    return query_blocks.reshape(seq_len, HQ * DH), accum[reach:].astype(jnp.bfloat16)


def reference(query, key_value, upstream, log_ratio, doc_starts, answer_counts):
    seq_len = query.shape[1]
    slot_count = doc_starts.shape[1]
    total_docs = jnp.sum((answer_counts > 0).astype(jnp.float32))
    positions = jnp.arange(seq_len, dtype=jnp.int32)
    slot_index = jnp.arange(slot_count, dtype=jnp.int32)
    query_out = []
    kv_out = []
    for sequence in range(query.shape[0]):
        starts = doc_starts[sequence].astype(jnp.int32)
        counts = answer_counts[sequence].astype(jnp.int32)
        doc_ends = jnp.concatenate([starts[1:], jnp.full((1,), seq_len, jnp.int32)])
        doc_of = doc_index(starts, positions)
        in_doc = doc_of[:, None] == slot_index[None, :]
        end_here = jnp.sum(jnp.where(in_doc, doc_ends[None, :], 0), axis=1)
        count_here = jnp.sum(jnp.where(in_doc, counts[None, :], 0), axis=1)
        answer = positions >= end_here - count_here
        picked = in_doc & answer[:, None]
        doc_sum = jnp.sum(jnp.where(picked, log_ratio[sequence][:, None], 0.0), axis=0)
        floored = jnp.maximum(counts, 1).astype(jnp.float32)
        doc_coef = LOSS_SCALE * 2.0 * jax.nn.sigmoid(doc_sum / floored) / (floored * total_docs)
        weight = jnp.sum(jnp.where(picked, doc_coef[None, :], 0.0), axis=1)
        out_grad = (weight[:, None] * upstream[sequence].astype(jnp.float32)).astype(jnp.bfloat16)
        query_grad, kv_grad = sequence_grads(query[sequence], key_value[sequence], out_grad, doc_of)
        query_out.append(query_grad)
        kv_out.append(kv_grad)
    return jnp.stack(query_out), jnp.stack(kv_out)
```

```python
from functools import partial

import jax
import jax.numpy as jnp
from jax import lax
from jax.experimental import pallas as pl
from jax.experimental.pallas import tpu as pltpu
from jax.sharding import PartitionSpec as P

HQ = 32
HK = 4
DH = 128
LOSS_SCALE = 65536
ROWS = 192
CHIP = 2 * ROWS
WIN = 3 * CHIP
GROUP = HQ // HK
SUB = 96
LANES = SUB * GROUP
SPANS = (256, 512, 640, 784, 896)
CHUNKS = 2
TAIL = 16
PACK = CHIP + 2 * TAIL
MASKED = -1e30
SCALE = DH ** (-0.5)
LOG2E = 1.4426950408889634
F32 = jnp.float32
BF16 = jnp.bfloat16


def to_column(row, shift=0):
    n = row.shape[1]
    r = lax.broadcasted_iota(jnp.int32, (n, n), 0)
    c = lax.broadcasted_iota(jnp.int32, (n, n), 1)
    return jnp.sum(jnp.where(c == r + shift, row, 0), axis=1, keepdims=True)


def end_row(starts, seq_len):
    n = starts.shape[1]
    r = lax.broadcasted_iota(jnp.int32, (n, n), 0)
    c = lax.broadcasted_iota(jnp.int32, (n, n), 1)
    col = to_column(starts)
    row = jnp.sum(jnp.where(r == c + 1, col, 0), axis=0, keepdims=True)
    lane = lax.broadcasted_iota(jnp.int32, (1, n), 1)
    return jnp.where(lane == n - 1, seq_len, row)


def prep_kernel(seq_len, idx_ref, kv_ref, lr_ref, st_ref, ct_ref, snd_ref, mine_ref):
    index = idx_ref[0]
    core = index % 2

    def put(dst, half):
        for j in range(CHUNKS):
            lo = half * CHUNKS * DH + j * DH
            dst[0:ROWS, 2 * j * DH : (2 * j + 1) * DH] = kv_ref[:, lo : lo + DH]
            dst[0:ROWS, (2 * j + 1) * DH : (2 * j + 2) * DH] = kv_ref[:, HK * DH + lo : HK * DH + lo + DH]

    for half in range(2):

        @pl.when(core == half)
        def _():
            put(mine_ref, half)
            put(snd_ref, 1 - half)

    starts = st_ref[...]
    n = starts.shape[1]
    row_i = lax.broadcasted_iota(jnp.int32, (n, 1), 0)
    st = to_column(starts)
    en = jnp.where(row_i == n - 1, seq_len, to_column(starts, 1))
    first = jnp.maximum(st, en - to_column(ct_ref[...]))
    pos = index * ROWS + lax.broadcasted_iota(jnp.int32, (n, ROWS), 1)
    part = jnp.sum(jnp.where((pos >= first) & (pos < en), lr_ref[...], 0.0), axis=1, keepdims=True)
    r = lax.broadcasted_iota(jnp.int32, (n, n), 0)
    c = lax.broadcasted_iota(jnp.int32, (n, n), 1)
    part = jnp.sum(jnp.where(r == c, part, 0.0), axis=0, keepdims=True)
    high = part.astype(BF16).astype(F32)
    rest = part - high
    mid = rest.astype(BF16).astype(F32)
    low = rest - mid
    k = lax.broadcasted_iota(jnp.int32, (TAIL, n), 0)
    tail = jnp.where(k == 0, high, jnp.where(k == 1, mid, jnp.where(k == 2, low, 0.0))).astype(BF16)
    for dst in (snd_ref, mine_ref):
        dst[ROWS : ROWS + TAIL, :] = jnp.zeros((TAIL, 2 * CHUNKS * DH), BF16)
        dst[ROWS : ROWS + TAIL, 0:n] = tail


def scalar_kernel(idx_ref, st_ref, ct_ref, sc_ref, cnt_ref):
    index = idx_ref[0]
    first = index // 2 * CHIP
    base = first - (WIN - CHIP)
    sc_ref[0] = index % 2
    sc_ref[1] = base
    n = st_ref.shape[0]

    def each(j, carry):
        lows = list(carry[:-1])
        start = st_ref[j]
        for s in range(CHIP // SUB):
            lows[s] = jnp.where(start <= first + s * SUB, start, lows[s])
        return (*lows, carry[-1] + (ct_ref[j] > 0).astype(jnp.int32))

    out = lax.fori_loop(0, n, each, (jnp.int32(0),) * (CHIP // SUB + 1))
    for s in range(CHIP // SUB):
        low = jnp.maximum(out[s] - base, 0) // 16 * 16
        need = (WIN - CHIP) + (s + 1) * SUB - low
        pick = jnp.int32(0)
        span = jnp.int32(SPANS[0])
        for v in range(1, len(SPANS)):
            more = need > SPANS[v - 1]
            pick = jnp.where(more, v, pick)
            span = jnp.where(more, SPANS[v], span)
        sc_ref[2 + 2 * s] = jnp.minimum(low, WIN - span)
        sc_ref[3 + 2 * s] = pick
    cnt_ref[...] = jnp.full(cnt_ref.shape, out[-1].astype(F32))


def nt(a, b):
    return lax.dot_general(a, b, (((1,), (1,)), ((), ())), preferred_element_type=F32)


def nn(a, b):
    return lax.dot_general(a, b, (((1,), (0,)), ((), ())), preferred_element_type=F32)


def tn(a, b):
    return lax.dot_general(a, b, (((0,), (0,)), ((), ())), preferred_element_type=F32)


def fold(x, op):
    out = x[0:8]
    for i in range(8, x.shape[0], 8):
        out = op(out, x[i : i + 8])
    return out


def attention_kernel(
    seq_len,
    sc_ref,
    q_ref,
    g_ref,
    qg_ref,
    own_ref,
    a_ref,
    b_ref,
    st_ref,
    ct_ref,
    dq_own_ref,
    dq_other_ref,
    d_own_ref,
    d_a_ref,
    d_b_ref,
    q_all,
    g_all,
    k_all,
    v_all,
    q_now,
    g_now,
    s_buf,
    d_buf,
    k_acc,
    v_acc,
    dq_all,
):
    core = sc_ref[0]
    base = sc_ref[1]
    mine = pl.multiple_of(core * ROWS, ROWS)
    other = pl.multiple_of((1 - core) * ROWS, ROWS)
    starts = st_ref[...]
    n = starts.shape[1]
    ends = end_row(starts, seq_len)
    first_answer = jnp.maximum(starts, ends - ct_ref[...])

    def answers(offset):
        pos = base + (WIN - CHIP) + offset + lax.broadcasted_iota(jnp.int32, (ROWS, n), 0)
        hit = jnp.where((pos >= first_answer) & (pos < ends), 1.0, 0.0)
        return jnp.sum(hit, axis=1, keepdims=True) > 0.5

    q_all[pl.ds(mine, ROWS), :] = q_ref[...]
    q_all[pl.ds(other, ROWS), :] = qg_ref[0]
    g_all[pl.ds(mine, ROWS), :] = jnp.where(answers(mine), g_ref[...], jnp.zeros((), BF16))
    g_all[pl.ds(other, ROWS), :] = jnp.where(answers(other), qg_ref[1], jnp.zeros((), BF16))
    for i, src in enumerate((b_ref, a_ref, own_ref)):
        for at, lo in ((mine, 0), (other, ROWS)):
            rows = pl.ds(i * CHIP + at, ROWS)
            k_all[rows, :] = src[lo : lo + ROWS, 0:DH]
            v_all[rows, :] = src[lo : lo + ROWS, DH : 2 * DH]
    k_acc[...] = jnp.zeros(k_acc.shape, F32)
    v_acc[...] = jnp.zeros(v_acc.shape, F32)
    st_col = to_column(starts)

    def span_step(span, key_first, row_first, low, pos):
        pieces = [(o, min(256, span - o)) for o in range(0, span, 256)]
        queries = q_now[...]
        grads = g_now[...]
        top = jnp.full((8, LANES), MASKED, F32)
        for o, size in pieces:
            at = pl.multiple_of(key_first + o, 16)
            scores = nt(k_all[pl.ds(at, size), :], queries)
            key_pos = base + at + lax.broadcasted_iota(jnp.int32, (size, LANES // 2), 0)
            seen = (key_pos >= low) & (key_pos <= pos)
            scores = jnp.where(jnp.concatenate([seen, seen], axis=1), scores, MASKED)
            s_buf[o : o + size, :] = scores
            top = jnp.maximum(top, fold(scores, jnp.maximum))
        peak = jnp.max(top, axis=0, keepdims=True) * (SCALE * LOG2E)
        total = jnp.zeros((8, LANES), F32)
        delta = jnp.zeros((8, LANES), F32)
        for o, size in pieces:
            at = pl.multiple_of(key_first + o, 16)
            d_probs = nt(v_all[pl.ds(at, size), :], grads)
            weight = jnp.exp2(s_buf[o : o + size, :] * (SCALE * LOG2E) - peak)
            s_buf[o : o + size, :] = weight
            d_buf[o : o + size, :] = d_probs
            total = total + fold(weight, jnp.add)
            delta = delta + fold(weight * d_probs, jnp.add)
        inverse = 1.0 / jnp.sum(total, axis=0, keepdims=True)
        delta = jnp.sum(delta, axis=0, keepdims=True) * inverse
        dq = None
        for o, size in pieces:
            at = pl.multiple_of(key_first + o, 16)
            rows = pl.ds(at, size)
            probs = s_buf[o : o + size, :] * inverse
            d_scores = (probs * (d_buf[o : o + size, :] - delta)).astype(BF16)
            v_acc[rows, :] += nn(probs.astype(BF16), grads)
            k_acc[rows, :] += nn(d_scores, queries)
            more = tn(d_scores, k_all[rows, :])
            dq = more if dq is None else dq + more
        dq = (dq * SCALE).astype(BF16)
        for h in range(GROUP):
            dq_all[pl.ds(row_first, SUB), h * DH : (h + 1) * DH] = dq[h * SUB : (h + 1) * SUB]

    def step(s, carry):
        key_first = pl.multiple_of(sc_ref[2 + 2 * s], 16)
        pick = sc_ref[3 + 2 * s]
        row_first = pl.multiple_of(s * SUB, SUB)
        for h in range(GROUP):
            q_now[h * SUB : (h + 1) * SUB, :] = q_all[pl.ds(row_first, SUB), h * DH : (h + 1) * DH]
            g_now[h * SUB : (h + 1) * SUB, :] = g_all[pl.ds(row_first, SUB), h * DH : (h + 1) * DH]
        lane = lax.broadcasted_iota(jnp.int32, (1, LANES // 2), 1)
        pos = base + (WIN - CHIP) + row_first + lane % SUB
        low = jnp.max(jnp.where(st_col <= pos, st_col, 0), axis=0, keepdims=True)
        for v, span in enumerate(SPANS):
            pl.when(pick == v)(partial(span_step, span, key_first, row_first, low, pos))
        return carry

    lax.fori_loop(0, CHIP // SUB, step, 0)
    dq_own_ref[...] = dq_all[pl.ds(mine, ROWS), :]
    dq_other_ref[...] = dq_all[pl.ds(other, ROWS), :]
    for i, dst in enumerate((d_b_ref, d_a_ref, d_own_ref)):
        for at, lo in ((mine, 0), (other, ROWS)):
            rows = pl.ds(i * CHIP + at, ROWS)
            dst[lo : lo + ROWS, 0:DH] = (k_acc[rows, :] * SCALE).astype(dst.dtype)
            dst[lo : lo + ROWS, DH : 2 * DH] = v_acc[rows, :].astype(dst.dtype)
    for dst in (d_b_ref, d_a_ref):
        dst[CHIP:PACK, :] = own_ref[CHIP:PACK, :]


def doc_coefs(seq_len, st_ref, ct_ref, cnt_refs, tail_refs):
    starts = st_ref[...]
    n = starts.shape[1]
    sums = jnp.zeros((1, n), F32)
    for ref in tail_refs:
        sums = sums + jnp.sum(ref[CHIP:PACK, 0:n].astype(F32), axis=0, keepdims=True)
    docs = cnt_refs[0][0:1, 0:n]
    for ref in cnt_refs[1:]:
        docs = docs + ref[0:1, 0:n]
    size = jnp.maximum(ct_ref[...], 1).astype(F32)
    coef = LOSS_SCALE * 2.0 / (1.0 + jnp.exp(-sums / size)) / (size * docs)
    return starts, end_row(starts, seq_len), coef


def row_coefs(starts, ends, coef, first):
    n = starts.shape[1]
    pos = first + lax.broadcasted_iota(jnp.int32, (ROWS, n), 0)
    return jnp.sum(jnp.where((pos >= starts) & (pos < ends), coef, 0.0), axis=1, keepdims=True)


def key_value_kernel(seq_len, idx_ref, st_ref, ct_ref, *refs):
    cnt_refs, fwd_refs = refs[0:4], refs[4:7]
    own_refs, a_refs, b_refs = refs[7:9], refs[9:11], refs[11:13]
    mine_ref, snd_ref = refs[13:15]
    index = idx_ref[0]
    starts, ends, coef = doc_coefs(seq_len, st_ref, ct_ref, cnt_refs, (*fwd_refs, a_refs[0], b_refs[0]))
    for dst, lo, where in ((mine_ref, 0, index), (snd_ref, ROWS, index // 2 * 2 + 1 - index % 2)):
        scale = row_coefs(starts, ends, coef, where * ROWS)
        for j in range(CHUNKS):
            rows = slice(lo, lo + ROWS)
            out = own_refs[j][rows, :] + a_refs[j][rows, :].astype(F32) + b_refs[j][rows, :].astype(F32)
            out = (out * scale).astype(BF16)
            dst[:, j * DH : (j + 1) * DH] = out[:, 0:DH]
            dst[:, (CHUNKS + j) * DH : (CHUNKS + j + 1) * DH] = out[:, DH : 2 * DH]


def query_kernel(seq_len, idx_ref, st_ref, ct_ref, *refs):
    cnt_refs, tail_refs = refs[0:4], refs[4:9]
    mine_refs, got_refs = refs[9:11], refs[11:13]
    out_ref = refs[13]
    index = idx_ref[0]
    starts, ends, coef = doc_coefs(seq_len, st_ref, ct_ref, cnt_refs, tail_refs)
    scale = row_coefs(starts, ends, coef, index * ROWS)
    width = GROUP * DH
    for half in range(2):

        @pl.when(index % 2 == half)
        def _():
            for k, srcs in ((half, mine_refs), (1 - half, got_refs)):
                for j in range(CHUNKS):
                    lo = (k * CHUNKS + j) * width
                    out_ref[:, lo : lo + width] = (srcs[j][...].astype(F32) * scale).astype(BF16)


def local(query, key_value, upstream, log_ratio, doc_starts, answer_counts):
    count = lax.axis_size("ctx")
    seq_len = ROWS * count
    index = lax.axis_index("ctx").astype(jnp.int32)
    core = index % 2
    where = index.reshape(1)
    smem = pl.BlockSpec(memory_space=pltpu.SMEM)
    vmem = pl.BlockSpec(memory_space=pltpu.VMEM)
    params = pltpu.CompilerParams(vmem_limit_bytes=56 << 20)

    def moved(value, steps):
        first, last = (max(0, -steps), min(count, count - steps))
        return lax.ppermute(value, "ctx", [(i, i + steps) for i in range(first, last)])

    def swapped(value):
        return lax.ppermute(value, "ctx", [(i, i ^ 1) for i in range(count)])

    def pallas(body, out_shape, in_specs, out_specs, name):
        return pl.pallas_call(
            body, out_shape=out_shape, in_specs=in_specs, out_specs=out_specs, compiler_params=params, name=name
        )

    shape = jax.ShapeDtypeStruct
    half_cols = CHUNKS * GROUP * DH
    packed = shape((ROWS + TAIL, 2 * CHUNKS * DH), BF16)
    snd, mine = pallas(
        partial(prep_kernel, seq_len), (packed, packed), [smem] + [vmem] * 4, (vmem, vmem), "prep"
    )(where, key_value[0], log_ratio, doc_starts, answer_counts)
    got = swapped(snd)
    own = []
    for j in range(CHUNKS):
        cols = slice(2 * j * DH, 2 * (j + 1) * DH)
        own.append(
            jnp.concatenate([mine[:ROWS, cols], got[:ROWS, cols], mine[ROWS:, cols], got[ROWS:, cols]], axis=0)
        )
    back1 = [moved(x, 2) for x in own]
    back2 = [moved(x, 4) for x in own]
    theirs = (1 - core) * half_cols
    to_send = jnp.stack(
        [
            lax.dynamic_slice_in_dim(query[0], theirs, half_cols, 1),
            lax.dynamic_slice_in_dim(upstream[0], theirs, half_cols, 1),
        ]
    )
    swapped_rows = swapped(to_send)
    scalars, docs = pallas(
        scalar_kernel,
        (shape((2 + 2 * (CHIP // SUB),), jnp.int32), shape((8, 128), F32)),
        [smem] * 3,
        (smem, vmem),
        "scalars",
    )(where, doc_starts[0], answer_counts[0])
    size = lax.axis_size("dp")
    docs_all = [docs] + [
        lax.ppermute(docs, "dp", [(i, (i + k) % size) for i in range(size)]) for k in range(1, size)
    ]

    width = GROUP * DH
    dq_mine, dq_other, d_own, d_a, d_b = [], [], [], [], []
    for j in range(CHUNKS):
        full = lambda i, sc: (0, 0)
        picked = lambda i, sc, j=j: (0, sc[0] * CHUNKS + j)
        pack_spec = pl.BlockSpec((PACK, 2 * DH), full)
        row_spec = pl.BlockSpec((1, doc_starts.shape[1]), full)
        outs = pl.pallas_call(
            partial(attention_kernel, seq_len),
            grid_spec=pltpu.PrefetchScalarGridSpec(
                num_scalar_prefetch=1,
                grid=(1,),
                in_specs=[
                    pl.BlockSpec((ROWS, width), picked),
                    pl.BlockSpec((ROWS, width), picked),
                    pl.BlockSpec((2, ROWS, width), lambda i, sc, j=j: (0, 0, j)),
                    pack_spec,
                    pack_spec,
                    pack_spec,
                    row_spec,
                    row_spec,
                ],
                out_specs=[
                    pl.BlockSpec((ROWS, width), full),
                    pl.BlockSpec((ROWS, width), full),
                    pl.BlockSpec((CHIP, 2 * DH), full),
                    pack_spec,
                    pack_spec,
                ],
                scratch_shapes=[
                    pltpu.VMEM((CHIP, width), BF16),
                    pltpu.VMEM((CHIP, width), BF16),
                    pltpu.VMEM((WIN, DH), BF16),
                    pltpu.VMEM((WIN, DH), BF16),
                    pltpu.VMEM((LANES, DH), BF16),
                    pltpu.VMEM((LANES, DH), BF16),
                    pltpu.VMEM((SPANS[-1], LANES), F32),
                    pltpu.VMEM((SPANS[-1], LANES), F32),
                    pltpu.VMEM((WIN, DH), F32),
                    pltpu.VMEM((WIN, DH), F32),
                    pltpu.VMEM((CHIP, width), BF16),
                ],
            ),
            out_shape=[
                shape((ROWS, width), BF16),
                shape((ROWS, width), BF16),
                shape((CHIP, 2 * DH), F32),
                shape((PACK, 2 * DH), BF16),
                shape((PACK, 2 * DH), BF16),
            ],
            compiler_params=params,
            name="attention",
        )(scalars, query[0], upstream[0], swapped_rows, own[j], back1[j], back2[j], doc_starts, answer_counts)
        for kept, out in zip((dq_mine, dq_other, d_own, d_a, d_b), outs):
            kept.append(out)

    got_a = [moved(x, -2) for x in d_a]
    got_b = [moved(x, -4) for x in d_b]
    dq_got = [swapped(x) for x in dq_other]
    half = shape((ROWS, 2 * CHUNKS * DH), BF16)
    kv_mine, kv_send = pallas(
        partial(key_value_kernel, seq_len), (half, half), [smem] + [vmem] * 15, (vmem, vmem), "kv_out"
    )(where, doc_starts, answer_counts, *docs_all, own[0], back1[0], back2[0], *d_own, *got_a, *got_b)
    kv_got = swapped(kv_send)
    d_query = pallas(
        partial(query_kernel, seq_len),
        shape((ROWS, HQ * DH), BF16),
        [smem] + [vmem] * 15,
        vmem,
        "q_out",
    )(where, doc_starts, answer_counts, *docs_all, own[0], back1[0], back2[0], got_a[0], got_b[0], *dq_mine, *dq_got)
    cut = CHUNKS * DH
    lower, upper = (jnp.where(core == 0, kv_mine, kv_got), jnp.where(core == 0, kv_got, kv_mine))
    d_key_value = jnp.concatenate([lower[:, :cut], upper[:, :cut], lower[:, cut:], upper[:, cut:]], axis=1)
    return (d_query[None], d_key_value[None])


def solution(mesh):
    return jax.shard_map(
        local,
        mesh=mesh,
        in_specs=(
            P("dp", "ctx", None),
            P("dp", "ctx", None),
            P("dp", "ctx", None),
            P("dp", "ctx"),
            P("dp", None),
            P("dp", None),
        ),
        out_specs=(P("dp", "ctx", None), P("dp", "ctx", None)),
        check_vma=False,
    )
```

```python
from functools import partial

import jax
import jax.numpy as jnp
from jax import lax
from jax.experimental import pallas as pl
from jax.experimental.pallas import tpu as pltpu
from jax.sharding import PartitionSpec as P


HQ = 32
HK = 4
DH = 128
LOSS_SCALE = 65536
ROWS = 192
CHIP = 2 * ROWS
WIN = 3 * CHIP
GROUP = HQ // HK
SUB = 96
LANES = SUB * GROUP
SPANS = (256, 512, 640, 784, 896)
CHUNKS = 2
TAIL = 16
PACK = CHIP + TAIL
MASKED = -1e30
SCALE = DH ** (-0.5)
LOG2E = 1.4426950408889634
DQ_T = True
KV_T = False
F32 = jnp.float32
BF16 = jnp.bfloat16


def to_column(row, shift=0):
    n = row.shape[1]
    r = lax.broadcasted_iota(jnp.int32, (n, n), 0)
    c = lax.broadcasted_iota(jnp.int32, (n, n), 1)
    return jnp.sum(jnp.where(c == r + shift, row, 0), axis=1, keepdims=True)


def end_row(starts, seq_len):
    n = starts.shape[1]
    r = lax.broadcasted_iota(jnp.int32, (n, n), 0)
    c = lax.broadcasted_iota(jnp.int32, (n, n), 1)
    col = to_column(starts)
    row = jnp.sum(jnp.where(r == c + 1, col, 0), axis=0, keepdims=True)
    lane = lax.broadcasted_iota(jnp.int32, (1, n), 1)
    return jnp.where(lane == n - 1, seq_len, row)


def pack_kernel(seq_len, idx_ref, kv_ref, got_ref, lr_ref, got_lr_ref, st_ref, ct_ref, *own_refs):
    index = idx_ref[0]
    core = index % 2
    for half in range(2):

        @pl.when(core == half)
        def _():
            for j in range(CHUNKS):
                for k in range(2):
                    lo = k * HK * DH + (half * CHUNKS + j) * DH
                    own_refs[j][0:ROWS, k * DH : (k + 1) * DH] = kv_ref[:, lo : lo + DH]
                    own_refs[j][ROWS:CHIP, k * DH : (k + 1) * DH] = got_ref[:, lo : lo + DH]

    starts = st_ref[...]
    n = starts.shape[1]
    row_i = lax.broadcasted_iota(jnp.int32, (n, 1), 0)
    st = to_column(starts)
    en = jnp.where(row_i == n - 1, seq_len, to_column(starts, 1))
    first = jnp.maximum(st, en - to_column(ct_ref[...]))
    lane = lax.broadcasted_iota(jnp.int32, (n, ROWS), 1)
    part = jnp.zeros((n, 1), F32)
    for ref, where in ((lr_ref, index), (got_lr_ref, index + 1 - 2 * core)):
        pos = where * ROWS + lane
        part = part + jnp.sum(jnp.where((pos >= first) & (pos < en), ref[...], 0.0), axis=1, keepdims=True)
    r = lax.broadcasted_iota(jnp.int32, (n, n), 0)
    c = lax.broadcasted_iota(jnp.int32, (n, n), 1)
    part = jnp.sum(jnp.where(r == c, part, 0.0), axis=0, keepdims=True)
    high = part.astype(BF16).astype(F32)
    rest = part - high
    mid = rest.astype(BF16).astype(F32)
    low = rest - mid
    k = lax.broadcasted_iota(jnp.int32, (TAIL, n), 0)
    tail = jnp.where(k == 0, high, jnp.where(k == 1, mid, jnp.where(k == 2, low, 0.0))).astype(BF16)
    for ref in own_refs:
        ref[CHIP:PACK, :] = jnp.zeros((TAIL, 2 * DH), BF16)
    own_refs[0][CHIP:PACK, 0:n] = tail


def early_kernel(idx_ref, q_hbm, g_hbm, kv_hbm, lr_ref, st_ref, ct_ref, sc_ref, cnt_ref, q_ref, g_ref, kv_ref, lr_out, st_out, ct_out, sems):
    cols = pl.ds(pl.multiple_of(idx_ref[0] % 2 * q_ref.shape[1], q_ref.shape[1]), q_ref.shape[1])
    copies = [
        pltpu.make_async_copy(kv_hbm, kv_ref, sems.at[0]),
        pltpu.make_async_copy(q_hbm.at[:, cols], q_ref, sems.at[1]),
        pltpu.make_async_copy(g_hbm.at[:, cols], g_ref, sems.at[2]),
    ]
    for copy in copies:
        copy.start()
    lr_out[...] = lr_ref[...]
    st_out[...] = st_ref[...]
    ct_out[...] = ct_ref[...]
    index = idx_ref[0]
    first = index // 2 * CHIP
    base = first - (WIN - CHIP)
    sc_ref[0] = index % 2
    sc_ref[1] = base
    starts = st_ref[...].astype(F32)
    for s in range(CHIP // SUB):
        at = (first + s * SUB).astype(F32)
        start = jnp.max(jnp.where(starts <= at, starts, 0.0)).astype(jnp.int32)
        low = jnp.maximum(start - base, 0) // 16 * 16
        need = (WIN - CHIP) + (s + 1) * SUB - low
        pick = jnp.int32(0)
        span = jnp.int32(SPANS[0])
        for v in range(1, len(SPANS)):
            more = need > SPANS[v - 1]
            pick = jnp.where(more, v, pick)
            span = jnp.where(more, SPANS[v], span)
        sc_ref[2 + 2 * s] = jnp.minimum(low, WIN - span)
        sc_ref[3 + 2 * s] = pick
    used = jnp.sum(jnp.where(ct_ref[...] > 0, 1.0, 0.0), axis=1, keepdims=True)
    cnt_ref[...] = jnp.broadcast_to(used, cnt_ref.shape)
    for copy in copies:
        copy.wait()


def nt(a, b):
    return lax.dot_general(a, b, (((1,), (1,)), ((), ())), preferred_element_type=F32)


def nn(a, b):
    return lax.dot_general(a, b, (((1,), (0,)), ((), ())), preferred_element_type=F32)


def tn(a, b):
    return lax.dot_general(a, b, (((0,), (0,)), ((), ())), preferred_element_type=F32)


def fold(x, op):
    out = x[0:8]
    for i in range(8, x.shape[0], 8):
        out = op(out, x[i : i + 8])
    return out


def attention_kernel(
    seq_len,
    chunk,
    sc_ref,
    q_ref,
    g_ref,
    got_q_ref,
    got_g_ref,
    own_ref,
    a_ref,
    b_ref,
    st_ref,
    ct_ref,
    dq_own_ref,
    dq_other_ref,
    d_own_ref,
    d_a_ref,
    d_b_ref,
    q_all,
    g_all,
    k_all,
    v_all,
    q_now,
    g_now,
    s_buf,
    d_buf,
    k_acc,
    v_acc,
    dq_all,
):
    core = sc_ref[0]
    base = sc_ref[1]
    mine = pl.multiple_of(core * ROWS, ROWS)
    other = pl.multiple_of((1 - core) * ROWS, ROWS)
    starts = st_ref[...]
    n = starts.shape[1]
    ends = end_row(starts, seq_len)
    first_answer = jnp.maximum(starts, ends - ct_ref[...])

    def answers(offset):
        pos = base + (WIN - CHIP) + offset + lax.broadcasted_iota(jnp.int32, (ROWS, n), 0)
        hit = jnp.where((pos >= first_answer) & (pos < ends), 1.0, 0.0)
        return jnp.sum(hit, axis=1, keepdims=True) > 0.5

    width = GROUP * DH
    cols = slice(chunk * width, (chunk + 1) * width)
    got_cols = pl.ds(pl.multiple_of((core * CHUNKS + chunk) * width, width), width)
    q_all[pl.ds(mine, ROWS), :] = q_ref[:, cols]
    q_all[pl.ds(other, ROWS), :] = got_q_ref[:, got_cols]
    g_all[pl.ds(mine, ROWS), :] = jnp.where(answers(mine), g_ref[:, cols], jnp.zeros((), BF16))
    g_all[pl.ds(other, ROWS), :] = jnp.where(answers(other), got_g_ref[:, got_cols], jnp.zeros((), BF16))
    for i, src in enumerate((b_ref, a_ref, own_ref)):
        for at, lo in ((mine, 0), (other, ROWS)):
            rows = pl.ds(i * CHIP + at, ROWS)
            k_all[rows, :] = src[lo : lo + ROWS, 0:DH]
            v_all[rows, :] = src[lo : lo + ROWS, DH : 2 * DH]
    k_acc[...] = jnp.zeros(k_acc.shape, F32)
    v_acc[...] = jnp.zeros(v_acc.shape, F32)
    st_col = to_column(starts)

    def span_step(span, key_first, row_first, low, pos):
        pieces = [(o, min(256, span - o)) for o in range(0, span, 256)]
        queries = q_now[...]
        grads = g_now[...]
        top = jnp.full((8, LANES), MASKED, F32)
        for o, size in pieces:
            at = pl.multiple_of(key_first + o, 16)
            scores = nt(k_all[pl.ds(at, size), :], queries)
            key_pos = base + at + lax.broadcasted_iota(jnp.int32, (size, LANES // 2), 0)
            seen = (key_pos >= low) & (key_pos <= pos)
            scores = jnp.where(jnp.concatenate([seen, seen], axis=1), scores, MASKED)
            s_buf[o : o + size, :] = scores
            top = jnp.maximum(top, fold(scores, jnp.maximum))
        peak = jnp.max(top, axis=0, keepdims=True) * (SCALE * LOG2E)
        total = jnp.zeros((8, LANES), F32)
        delta = jnp.zeros((8, LANES), F32)
        for o, size in pieces:
            at = pl.multiple_of(key_first + o, 16)
            d_probs = nt(v_all[pl.ds(at, size), :], grads)
            weight = jnp.exp2(s_buf[o : o + size, :] * (SCALE * LOG2E) - peak)
            s_buf[o : o + size, :] = weight
            d_buf[o : o + size, :] = d_probs
            total = total + fold(weight, jnp.add)
            delta = delta + fold(weight * d_probs, jnp.add)
        inverse = 1.0 / jnp.sum(total, axis=0, keepdims=True)
        delta = jnp.sum(delta, axis=0, keepdims=True) * inverse
        dq = None
        grads_t = grads.T if KV_T else None
        queries_t = queries.T if KV_T else None
        for o, size in pieces:
            at = pl.multiple_of(key_first + o, 16)
            rows = pl.ds(at, size)
            probs = s_buf[o : o + size, :] * inverse
            d_scores = (probs * (d_buf[o : o + size, :] - delta)).astype(BF16)
            if KV_T:
                v_acc[rows, :] += nt(grads_t, probs.astype(BF16)).T
                k_acc[rows, :] += nt(queries_t, d_scores).T
            else:
                v_acc[rows, :] += nn(probs.astype(BF16), grads)
                k_acc[rows, :] += nn(d_scores, queries)
            more = tn(k_all[rows, :], d_scores) if DQ_T else tn(d_scores, k_all[rows, :])
            dq = more if dq is None else dq + more
        if DQ_T:
            dq = dq.T
        dq = (dq * SCALE).astype(BF16)
        for h in range(GROUP):
            dq_all[pl.ds(row_first, SUB), h * DH : (h + 1) * DH] = dq[h * SUB : (h + 1) * SUB]

    def step(s, carry):
        key_first = pl.multiple_of(sc_ref[2 + 2 * s], 16)
        pick = sc_ref[3 + 2 * s]
        row_first = pl.multiple_of(s * SUB, SUB)
        for h in range(GROUP):
            q_now[h * SUB : (h + 1) * SUB, :] = q_all[pl.ds(row_first, SUB), h * DH : (h + 1) * DH]
            g_now[h * SUB : (h + 1) * SUB, :] = g_all[pl.ds(row_first, SUB), h * DH : (h + 1) * DH]
        lane = lax.broadcasted_iota(jnp.int32, (1, LANES // 2), 1)
        pos = base + (WIN - CHIP) + row_first + lane % SUB
        low = jnp.max(jnp.where(st_col <= pos, st_col, 0), axis=0, keepdims=True)
        for v, span in enumerate(SPANS):
            pl.when(pick == v)(partial(span_step, span, key_first, row_first, low, pos))
        return carry

    lax.fori_loop(0, CHIP // SUB, step, 0)
    dq_own_ref[...] = dq_all[pl.ds(mine, ROWS), :]
    dq_other_ref[...] = dq_all[pl.ds(other, ROWS), :]
    for i, dst in enumerate((d_b_ref, d_a_ref, d_own_ref)):
        for at, lo in ((mine, 0), (other, ROWS)):
            rows = pl.ds(i * CHIP + at, ROWS)
            dst[lo : lo + ROWS, 0:DH] = (k_acc[rows, :] * SCALE).astype(dst.dtype)
            dst[lo : lo + ROWS, DH : 2 * DH] = v_acc[rows, :].astype(dst.dtype)
    for dst in (d_b_ref, d_a_ref):
        dst[CHIP:PACK, :] = own_ref[CHIP:PACK, :]


def row_coefs(starts, ends, coef, first):
    n = starts.shape[1]
    pos = first + lax.broadcasted_iota(jnp.int32, (ROWS, n), 0)
    return jnp.sum(jnp.where((pos >= starts) & (pos < ends), coef, 0.0), axis=1, keepdims=True)


def query_kernel(seq_len, idx_ref, st_ref, ct_ref, docs_ref, more_ref, *refs):
    tail_refs, mine_refs, got_refs = refs[0:5], refs[5:7], refs[7:9]
    out_ref, scale_ref, other_ref = refs[9:12]
    index = idx_ref[0]
    step = pl.program_id(0)

    @pl.when(step == 0)
    def _():
        starts = st_ref[...]
        n = starts.shape[1]
        sums = jnp.zeros((1, n), F32)
        for ref in tail_refs:
            sums = sums + jnp.sum(ref[CHIP:PACK, 0:n].astype(F32), axis=0, keepdims=True)
        size = jnp.maximum(ct_ref[...], 1).astype(F32)
        coef = LOSS_SCALE * 2.0 / (1.0 + jnp.exp(-sums / size)) / (size * (docs_ref[0:1, 0:n] + more_ref[0:1, 0:n]))
        ends = end_row(starts, seq_len)
        for dst, where in ((scale_ref, index), (other_ref, index // 2 * 2 + 1 - index % 2)):
            dst[...] = jnp.broadcast_to(row_coefs(starts, ends, coef, where * ROWS), dst.shape)

    scale = scale_ref[:, 0:1]
    for k, srcs in ((0, mine_refs), (1, got_refs)):
        for j in range(CHUNKS):

            @pl.when(step == (index % 2 + k) % 2 * CHUNKS + j)
            def _():
                out_ref[...] = (srcs[j][...].astype(F32) * scale).astype(BF16)


def key_value_kernel(*refs):
    scale_refs, own_refs, a_refs, b_refs, outs = refs[0:2], refs[2:4], refs[4:6], refs[6:8], refs[8:10]
    for i in range(2):
        rows = slice(i * ROWS, (i + 1) * ROWS)
        scale = scale_refs[i][...]
        for j in range(CHUNKS):
            for k in range(2):
                cols = slice(k * DH, (k + 1) * DH)
                out = own_refs[j][rows, cols] + a_refs[j][rows, cols].astype(F32) + b_refs[j][rows, cols].astype(F32)
                at = (k * CHUNKS + j) * DH
                outs[i][:, at : at + DH] = (out * scale).astype(BF16)


def in_vmem(x):
    return pltpu.with_memory_space_constraint(x, pltpu.VMEM)


def in_hbm(x):
    return pltpu.with_memory_space_constraint(x, pltpu.HBM)


def local(query, key_value, upstream, log_ratio, doc_starts, answer_counts):
    count = lax.axis_size("ctx")
    seq_len = ROWS * count
    index = lax.axis_index("ctx").astype(jnp.int32)
    core = index % 2
    where = index.reshape(1)
    smem = pl.BlockSpec(memory_space=pltpu.SMEM)
    vmem = pl.BlockSpec(memory_space=pltpu.VMEM)

    def moved(value, steps):
        first, last = (max(0, -steps), min(count, count - steps))
        return lax.ppermute(value, "ctx", [(i, i + steps) for i in range(first, last)])

    def swapped(value):
        return lax.ppermute(value, "ctx", [(i, i ^ 1) for i in range(count)])

    def exchanged(value, bit):
        return lax.ppermute(value, "dp", [(i, i ^ bit) for i in range(lax.axis_size("dp"))])

    width = GROUP * DH
    got_lr = swapped(log_ratio)
    got_kv = swapped(key_value[0])
    hbm = pl.BlockSpec(memory_space=pl.ANY)
    half_cols = CHUNKS * width
    slots = doc_starts.shape[1]
    scalars, docs, own_q, own_g, own_kv, ratios, starts, counts = pl.pallas_call(
        early_kernel,
        out_shape=(
            jax.ShapeDtypeStruct((2 + 2 * (CHIP // SUB),), jnp.int32),
            pltpu.VMEM((8, 128), F32),
            pltpu.VMEM((ROWS, half_cols), BF16),
            pltpu.VMEM((ROWS, half_cols), BF16),
            pltpu.VMEM((ROWS, 2 * HK * DH), BF16),
            pltpu.VMEM((1, ROWS), F32),
            pltpu.VMEM((1, slots), jnp.int32),
            pltpu.VMEM((1, slots), jnp.int32),
        ),
        in_specs=[smem] + [hbm] * 3 + [vmem] * 3,
        out_specs=(smem,) + (vmem,) * 7,
        scratch_shapes=[pltpu.SemaphoreType.DMA((3,))],
        compiler_params=pltpu.CompilerParams(vmem_limit_bytes=4 << 20),
        name="early",
    )(where, *[in_hbm(x) for x in (query[0], upstream[0], key_value[0], log_ratio, doc_starts, answer_counts)])
    packed = pltpu.VMEM((PACK, 2 * DH), BF16)
    own = pl.pallas_call(
        partial(pack_kernel, seq_len),
        out_shape=(packed,) * CHUNKS,
        in_specs=[smem] + [vmem] * 6,
        out_specs=(vmem,) * CHUNKS,
        compiler_params=pltpu.CompilerParams(vmem_limit_bytes=4 << 20),
        name="pack",
    )(where, *[in_vmem(x) for x in (own_kv, got_kv, ratios, got_lr, starts, counts)])
    back1, back2 = [], []
    for j in range(CHUNKS):
        back1.append(moved(own[j], 2))
        back2.append(moved(own[j], 4))
    got_q = swapped(query[0])
    got_g = swapped(upstream[0])
    more_docs = exchanged(docs, 1)

    dq_mine, dq_other, d_own, d_a, d_b = [], [], [], [], []
    for j in range(CHUNKS):
        operands = (own_q, own_g, got_q, got_g, own[j], back1[j], back2[j], starts, counts)
        outs = pl.pallas_call(
            partial(attention_kernel, seq_len, j),
            in_specs=[smem] + [vmem] * 9,
            out_specs=[vmem] * 5,
            scratch_shapes=[
                pltpu.VMEM((CHIP, width), BF16),
                pltpu.VMEM((CHIP, width), BF16),
                pltpu.VMEM((WIN, DH), BF16),
                pltpu.VMEM((WIN, DH), BF16),
                pltpu.VMEM((LANES, DH), BF16),
                pltpu.VMEM((LANES, DH), BF16),
                pltpu.VMEM((SPANS[-1], LANES), F32),
                pltpu.VMEM((SPANS[-1], LANES), F32),
                pltpu.VMEM((WIN, DH), F32),
                pltpu.VMEM((WIN, DH), F32),
                pltpu.VMEM((CHIP, width), BF16),
            ],
            out_shape=[
                pltpu.VMEM((ROWS, width), BF16),
                pltpu.VMEM((ROWS, width), BF16),
                pltpu.VMEM((CHIP, 2 * DH), F32),
                pltpu.VMEM((PACK, 2 * DH), BF16),
                pltpu.VMEM((PACK, 2 * DH), BF16),
            ],
            compiler_params=pltpu.CompilerParams(vmem_limit_bytes=24 << 20),
        )(scalars, *[in_vmem(x) for x in operands])
        for kept, out in zip((dq_mine, dq_other, d_own, d_a, d_b), outs):
            kept.append(out)

    got_a, got_b, dq_got = [], [], []
    for j in range(CHUNKS):
        got_a.append(moved(d_a[j], -2))
        got_b.append(moved(d_b[j], -4))
        dq_got.append(swapped(dq_other[j]))
    docs = docs + more_docs
    more_docs = exchanged(docs, 2)
    tails = (own[0], back1[0], back2[0], got_a[0], got_b[0])
    d_query, scale_mine, scale_other = pl.pallas_call(
        partial(query_kernel, seq_len),
        grid=(2 * CHUNKS,),
        out_shape=(
            jax.ShapeDtypeStruct((ROWS, HQ * DH), BF16),
            pltpu.VMEM((ROWS, DH), F32),
            pltpu.VMEM((ROWS, DH), F32),
        ),
        in_specs=[smem] + [vmem] * 13,
        out_specs=(pl.BlockSpec((ROWS, width), lambda i: (0, i)), vmem, vmem),
        compiler_params=pltpu.CompilerParams(vmem_limit_bytes=8 << 20),
        name="q_out",
    )(where, *[in_vmem(x) for x in (starts, counts, docs, more_docs, *tails, *dq_mine, *dq_got)])
    half = pltpu.VMEM((ROWS, 2 * CHUNKS * DH), BF16)
    kv_mine, kv_send = pl.pallas_call(
        key_value_kernel,
        out_shape=(half, half),
        in_specs=[vmem] * 8,
        out_specs=(vmem, vmem),
        compiler_params=pltpu.CompilerParams(vmem_limit_bytes=4 << 20),
        name="kv_out",
    )(*[in_vmem(x) for x in (scale_mine, scale_other, *d_own, *got_a, *got_b)])
    kv_got = swapped(kv_send)
    cut = CHUNKS * DH
    lower, upper = (jnp.where(core == 0, kv_mine, kv_got), jnp.where(core == 0, kv_got, kv_mine))
    d_key_value = jnp.concatenate([lower[:, :cut], upper[:, :cut], lower[:, cut:], upper[:, cut:]], axis=1)
    return (d_query[None], d_key_value[None])


def solution(mesh):
    return jax.shard_map(
        local,
        mesh=mesh,
        in_specs=(
            P("dp", "ctx", None),
            P("dp", "ctx", None),
            P("dp", "ctx", None),
            P("dp", "ctx"),
            P("dp", None),
            P("dp", None),
        ),
        out_specs=(P("dp", "ctx", None), P("dp", "ctx", None)),
        check_vma=False,
    )
```

```python
from functools import partial

import jax
import jax.numpy as jnp
from jax import lax
from jax.experimental import pallas as pl
from jax.experimental.pallas import tpu as pltpu
from jax.sharding import PartitionSpec as P


HQ = 32
HK = 4
DH = 128
LOSS_SCALE = 65536
ROWS = 192
CHIP = 2 * ROWS
WIN = 3 * CHIP
GROUP = HQ // HK
SUB = 96
LANES = SUB * GROUP
SPANS = (256, 512, 640, 704, 784, 896)
CHUNKS = 2
TAIL = 16
PACK = CHIP + TAIL
MASKED = -1e30
SCALE = DH ** (-0.5)
LOG2E = 1.4426950408889634
HALVES = 1
PART = LANES // HALVES
SHARED = 384
F32 = jnp.float32
BF16 = jnp.bfloat16


def to_column(row, shift=0):
    n = row.shape[1]
    r = lax.broadcasted_iota(jnp.int32, (n, n), 0)
    c = lax.broadcasted_iota(jnp.int32, (n, n), 1)
    return jnp.sum(jnp.where(c == r + shift, row, 0), axis=1, keepdims=True)


def end_row(starts, seq_len):
    n = starts.shape[1]
    r = lax.broadcasted_iota(jnp.int32, (n, n), 0)
    c = lax.broadcasted_iota(jnp.int32, (n, n), 1)
    col = to_column(starts)
    row = jnp.sum(jnp.where(r == c + 1, col, 0), axis=0, keepdims=True)
    lane = lax.broadcasted_iota(jnp.int32, (1, n), 1)
    return jnp.where(lane == n - 1, seq_len, row)


def pack_kernel(seq_len, idx_ref, kv_ref, got_ref, lr_ref, got_lr_ref, st_ref, ct_ref, *own_refs):
    index = idx_ref[0]
    core = index % 2
    for half in range(2):

        @pl.when(core == half)
        def _():
            for j in range(CHUNKS):
                for k in range(2):
                    lo = k * HK * DH + (half * CHUNKS + j) * DH
                    own_refs[j][0:ROWS, k * DH : (k + 1) * DH] = kv_ref[:, lo : lo + DH]
                    own_refs[j][ROWS:CHIP, k * DH : (k + 1) * DH] = got_ref[:, lo : lo + DH]

    starts = st_ref[...]
    n = starts.shape[1]
    row_i = lax.broadcasted_iota(jnp.int32, (n, 1), 0)
    st = to_column(starts)
    en = jnp.where(row_i == n - 1, seq_len, to_column(starts, 1))
    first = jnp.maximum(st, en - to_column(ct_ref[...]))
    lane = lax.broadcasted_iota(jnp.int32, (n, ROWS), 1)
    part = jnp.zeros((n, 1), F32)
    for ref, where in ((lr_ref, index), (got_lr_ref, index + 1 - 2 * core)):
        pos = where * ROWS + lane
        part = part + jnp.sum(jnp.where((pos >= first) & (pos < en), ref[...], 0.0), axis=1, keepdims=True)
    r = lax.broadcasted_iota(jnp.int32, (n, n), 0)
    c = lax.broadcasted_iota(jnp.int32, (n, n), 1)
    part = jnp.sum(jnp.where(r == c, part, 0.0), axis=0, keepdims=True)
    high = part.astype(BF16).astype(F32)
    rest = part - high
    mid = rest.astype(BF16).astype(F32)
    low = rest - mid
    k = lax.broadcasted_iota(jnp.int32, (TAIL, n), 0)
    tail = jnp.where(k == 0, high, jnp.where(k == 1, mid, jnp.where(k == 2, low, 0.0))).astype(BF16)
    for ref in own_refs:
        ref[CHIP:PACK, :] = jnp.zeros((TAIL, 2 * DH), BF16)
    own_refs[0][CHIP:PACK, 0:n] = tail


def early_kernel(kv_hbm, lr_ref, st_ref, ct_ref, kv_ref, lr_out, st_out, ct_out, sem):
    copy = pltpu.make_async_copy(kv_hbm, kv_ref, sem)
    copy.start()
    lr_out[...] = lr_ref[...]
    st_out[...] = st_ref[...]
    ct_out[...] = ct_ref[...]
    copy.wait()


def join_kernel(seq_len, idx_ref, q_hbm, g_hbm, got_q_ref, got_g_ref, st_ref, ct_ref, sc_ref, cnt_ref, q_all, g_all, sems):
    core = idx_ref[0] % 2
    width = q_all.shape[1]
    cols = pl.ds(pl.multiple_of(core * width, width), width)
    mine = pl.ds(pl.multiple_of(core * ROWS, ROWS), ROWS)
    other = pl.ds(pl.multiple_of((1 - core) * ROWS, ROWS), ROWS)
    copies = [
        pltpu.make_async_copy(q_hbm.at[:, cols], q_all.at[mine], sems.at[0]),
        pltpu.make_async_copy(g_hbm.at[:, cols], g_all.at[mine], sems.at[1]),
    ]
    for copy in copies:
        copy.start()
    index = idx_ref[0]
    first = index // 2 * CHIP
    base = first - (WIN - CHIP)
    sc_ref[0] = index % 2
    sc_ref[1] = base
    starts = st_ref[...].astype(F32)
    for s in range(CHIP // SUB):
        at = (first + s * SUB).astype(F32)
        start = jnp.max(jnp.where(starts <= at, starts, 0.0)).astype(jnp.int32)
        low = jnp.maximum(start - base, 0) // 16 * 16
        need = (WIN - CHIP) + (s + 1) * SUB - low
        pick = jnp.int32(0)
        span = jnp.int32(SPANS[0])
        for v in range(1, len(SPANS)):
            more = need > SPANS[v - 1]
            pick = jnp.where(more, v, pick)
            span = jnp.where(more, SPANS[v], span)
        sc_ref[2 + 2 * s] = jnp.minimum(low, WIN - span)
        sc_ref[3 + 2 * s] = pick
    used = jnp.sum(jnp.where(ct_ref[...] > 0, 1.0, 0.0), axis=1, keepdims=True)
    cnt_ref[...] = jnp.broadcast_to(used, cnt_ref.shape)
    slots = st_ref[...]
    ends = end_row(slots, seq_len)
    first_answer = jnp.maximum(slots, ends - ct_ref[...])

    def answers(where):
        pos = where * ROWS + lax.broadcasted_iota(jnp.int32, (ROWS, slots.shape[1]), 0)
        hit = jnp.where((pos >= first_answer) & (pos < ends), 1.0, 0.0)
        return jnp.sum(hit, axis=1, keepdims=True) > 0.5

    q_all[other, :] = got_q_ref[:, cols]
    g_all[other, :] = jnp.where(answers(index + 1 - 2 * core), got_g_ref[:, cols], jnp.zeros((), BF16))
    kept = answers(index)
    for copy in copies:
        copy.wait()
    g_all[mine, :] = jnp.where(kept, g_all[mine, :], jnp.zeros((), BF16))


def nt(a, b):
    return lax.dot_general(a, b, (((1,), (1,)), ((), ())), preferred_element_type=F32)


def nn(a, b):
    return lax.dot_general(a, b, (((1,), (0,)), ((), ())), preferred_element_type=F32)


def tn(a, b):
    return lax.dot_general(a, b, (((0,), (0,)), ((), ())), preferred_element_type=F32)


def fold(x, op):
    out = x[0:8]
    for i in range(8, x.shape[0], 8):
        out = op(out, x[i : i + 8])
    return out


def attention_kernel(chunk, sc_ref, q_all, g_all, own_ref, a_ref, b_ref, st_ref, *refs):
    refs = refs[1:] if chunk else refs
    dq_own_ref, dq_other_ref, d_own_ref, d_a_ref, d_b_ref, *refs = refs
    k_all, v_all, q_now, g_now, s_buf, d_buf, k_acc, v_acc, dq_now, dq_all = refs
    core = sc_ref[0]
    base = sc_ref[1]
    mine = pl.multiple_of(core * ROWS, ROWS)
    other = pl.multiple_of((1 - core) * ROWS, ROWS)
    width = GROUP * DH
    for i, src in enumerate((b_ref, a_ref, own_ref)):
        for at, lo in ((mine, 0), (other, ROWS)):
            rows = pl.ds(i * CHIP + at, ROWS)
            k_all[rows, :] = src[lo : lo + ROWS, 0:DH]
            v_all[rows, :] = src[lo : lo + ROWS, DH : 2 * DH]
    k_acc[...] = jnp.zeros(k_acc.shape, F32)
    v_acc[...] = jnp.zeros(v_acc.shape, F32)
    starts = st_ref[...]
    st_col = to_column(starts)

    def flush(row_first):
        done = dq_now[...].T
        for h in range(GROUP):
            dq_all[pl.ds(row_first, SUB), h * DH : (h + 1) * DH] = done[h * SUB : (h + 1) * SUB].astype(BF16)

    def span_step(span, key_first, row_first, low, pos):
        pieces = [(o, min(256, span - o)) for o in range(0, span, 256)]
        flush(row_first)
        state = [{} for _ in range(HALVES)]

        def rows_of(o, size):
            return pl.ds(pl.multiple_of(key_first + o, 16), size)

        def score(i, o, size):
            part = slice(i * PART, (i + 1) * PART)
            scores = nt(k_all[rows_of(o, size), :], q_now[part, :])
            key_pos = base + key_first + o + lax.broadcasted_iota(jnp.int32, (size, SHARED), 0)
            seen = (key_pos >= low) & (key_pos <= pos)
            scores = jnp.where(jnp.concatenate([seen] * (PART // SHARED), axis=1), scores, MASKED)
            s_buf[o : o + size, part] = scores
            top = fold(scores, jnp.maximum)
            state[i]["top"] = top if o == 0 else jnp.maximum(state[i]["top"], top)

        def weigh(i, o, size):
            part = slice(i * PART, (i + 1) * PART)
            if o == 0:
                state[i]["peak"] = jnp.max(state[i]["top"], axis=0, keepdims=True) * (SCALE * LOG2E)
            d_probs = nt(v_all[rows_of(o, size), :], g_now[part, :])
            weight = jnp.exp2(s_buf[o : o + size, part] * (SCALE * LOG2E) - state[i]["peak"])
            s_buf[o : o + size, part] = weight
            d_buf[o : o + size, part] = d_probs
            total = fold(weight, jnp.add)
            delta = fold(weight * d_probs, jnp.add)
            state[i]["total"] = total if o == 0 else state[i]["total"] + total
            state[i]["delta"] = delta if o == 0 else state[i]["delta"] + delta

        def finish(i, o, size):
            part = slice(i * PART, (i + 1) * PART)
            if o == 0:
                inverse = 1.0 / jnp.sum(state[i]["total"], axis=0, keepdims=True)
                state[i]["inverse"] = inverse
                state[i]["delta"] = jnp.sum(state[i]["delta"], axis=0, keepdims=True) * inverse
            rows = rows_of(o, size)
            probs = s_buf[o : o + size, part] * state[i]["inverse"]
            d_scores = (probs * (d_buf[o : o + size, part] - state[i]["delta"])).astype(BF16)
            v_acc[rows, :] += nn(probs.astype(BF16), g_now[part, :])
            k_acc[rows, :] += nn(d_scores, q_now[part, :])
            dq = tn(k_all[rows, :], d_scores)
            state[i]["dq"] = dq if o == 0 else state[i]["dq"] + dq

        stages = (score, weigh, finish)
        for t in range(len(stages) + HALVES - 1):
            for o, size in pieces:
                for i in range(HALVES):
                    if 0 <= t - i < len(stages):
                        stages[t - i](i, o, size)
        for i in range(HALVES):
            dq_now[:, i * PART : (i + 1) * PART] = state[i]["dq"] * SCALE

    def step(s, carry):
        key_first = pl.multiple_of(sc_ref[2 + 2 * s], 16)
        pick = sc_ref[3 + 2 * s]
        row_first = pl.multiple_of(s * SUB, SUB)
        for h in range(GROUP):
            col = chunk * width + h * DH
            q_now[h * SUB : (h + 1) * SUB, :] = q_all[pl.ds(row_first, SUB), col : col + DH]
            g_now[h * SUB : (h + 1) * SUB, :] = g_all[pl.ds(row_first, SUB), col : col + DH]
        lane = lax.broadcasted_iota(jnp.int32, (1, SHARED), 1)
        pos = base + (WIN - CHIP) + row_first + lane % SUB
        low = jnp.max(jnp.where(st_col <= pos, st_col, 0), axis=0, keepdims=True)
        for v, span in enumerate(SPANS):
            pl.when(pick == v)(partial(span_step, span, key_first, row_first, low, pos))
        return carry

    lax.fori_loop(0, CHIP // SUB, step, 0)
    flush(CHIP)
    dq_own_ref[...] = dq_all[pl.ds(SUB + mine, ROWS), :]
    dq_other_ref[:, chunk * width : (chunk + 1) * width] = dq_all[pl.ds(SUB + other, ROWS), :]
    for i, dst in enumerate((d_b_ref, d_a_ref, d_own_ref)):
        for at, lo in ((mine, 0), (other, ROWS)):
            rows = pl.ds(i * CHIP + at, ROWS)
            dst[lo : lo + ROWS, 0:DH] = (k_acc[rows, :] * SCALE).astype(dst.dtype)
            dst[lo : lo + ROWS, DH : 2 * DH] = v_acc[rows, :].astype(dst.dtype)
    d_b_ref[CHIP:PACK, 0:DH] = own_ref[CHIP:PACK, 0:DH]
    d_b_ref[CHIP:PACK, DH : 2 * DH] = a_ref[CHIP:PACK, 0:DH]


def row_coefs(starts, ends, coef, first):
    n = starts.shape[1]
    pos = first + lax.broadcasted_iota(jnp.int32, (ROWS, n), 0)
    return jnp.sum(jnp.where((pos >= starts) & (pos < ends), coef, 0.0), axis=1, keepdims=True)


def query_kernel(seq_len, idx_ref, st_ref, ct_ref, docs_ref, more_ref, *refs):
    tail_refs, mine_refs, got_ref = refs[0:4], refs[4:6], refs[6]
    out_ref, scale_ref, other_ref = refs[7:10]
    index = idx_ref[0]
    step = pl.program_id(0)

    @pl.when(step == 0)
    def _():
        starts = st_ref[...]
        n = starts.shape[1]
        sums = jnp.zeros((1, n), F32)
        for ref in tail_refs:
            sums = sums + jnp.sum(ref[CHIP:PACK, 0:n].astype(F32), axis=0, keepdims=True)
        sums = sums + jnp.sum(tail_refs[-1][CHIP:PACK, DH : DH + n].astype(F32), axis=0, keepdims=True)
        size = jnp.maximum(ct_ref[...], 1).astype(F32)
        coef = LOSS_SCALE * 2.0 / (1.0 + jnp.exp(-sums / size)) / (size * (docs_ref[0:1, 0:n] + more_ref[0:1, 0:n]))
        ends = end_row(starts, seq_len)
        for dst, where in ((scale_ref, index), (other_ref, index // 2 * 2 + 1 - index % 2)):
            dst[...] = jnp.broadcast_to(row_coefs(starts, ends, coef, where * ROWS), dst.shape)

    scale = scale_ref[:, 0:1]
    width = GROUP * DH
    for k in range(2):
        for j in range(CHUNKS):

            @pl.when(step == (index % 2 + k) % 2 * CHUNKS + j)
            def _():
                src = got_ref[:, j * width : (j + 1) * width] if k else mine_refs[j][...]
                out_ref[...] = (src.astype(F32) * scale).astype(BF16)


def key_value_kernel(*refs):
    scale_refs, own_refs, a_refs, b_refs, outs = refs[0:2], refs[2:4], refs[4:6], refs[6:8], refs[8:10]
    for i in range(2):
        rows = slice(i * ROWS, (i + 1) * ROWS)
        scale = scale_refs[i][...]
        for j in range(CHUNKS):
            for k in range(2):
                cols = slice(k * DH, (k + 1) * DH)
                out = own_refs[j][rows, cols] + a_refs[j][rows, cols].astype(F32) + b_refs[j][rows, cols].astype(F32)
                at = (k * CHUNKS + j) * DH
                outs[i][:, at : at + DH] = (out * scale).astype(BF16)


def in_vmem(x):
    return pltpu.with_memory_space_constraint(x, pltpu.VMEM)


def in_hbm(x):
    return pltpu.with_memory_space_constraint(x, pltpu.HBM)


def local(query, key_value, upstream, log_ratio, doc_starts, answer_counts):
    count = lax.axis_size("ctx")
    seq_len = ROWS * count
    index = lax.axis_index("ctx").astype(jnp.int32)
    core = index % 2
    where = index.reshape(1)
    smem = pl.BlockSpec(memory_space=pltpu.SMEM)
    vmem = pl.BlockSpec(memory_space=pltpu.VMEM)

    def moved(value, steps):
        return lax.ppermute(value, "ctx", [(i, (i + steps) % count) for i in range(count)])

    def swapped(value):
        return lax.ppermute(value, "ctx", [(i, i ^ 1) for i in range(count)])

    def exchanged(value, bit):
        return lax.ppermute(value, "dp", [(i, i ^ bit) for i in range(lax.axis_size("dp"))])

    width = GROUP * DH
    got_lr = swapped(log_ratio)
    got_kv = swapped(key_value[0])
    hbm = pl.BlockSpec(memory_space=pl.ANY)
    slots = doc_starts.shape[1]
    own_kv, ratios, starts, counts = pl.pallas_call(
        early_kernel,
        out_shape=(
            pltpu.VMEM((ROWS, 2 * HK * DH), BF16),
            pltpu.VMEM((1, ROWS), F32),
            pltpu.VMEM((1, slots), jnp.int32),
            pltpu.VMEM((1, slots), jnp.int32),
        ),
        in_specs=[hbm] + [vmem] * 3,
        out_specs=(vmem,) * 4,
        scratch_shapes=[pltpu.SemaphoreType.DMA],
        compiler_params=pltpu.CompilerParams(vmem_limit_bytes=4 << 20),
        name="early",
    )(*[in_hbm(x) for x in (key_value[0], log_ratio, doc_starts, answer_counts)])
    packed = pltpu.VMEM((PACK, 2 * DH), BF16)
    own = pl.pallas_call(
        partial(pack_kernel, seq_len),
        out_shape=(packed,) * CHUNKS,
        in_specs=[smem] + [vmem] * 6,
        out_specs=(vmem,) * CHUNKS,
        compiler_params=pltpu.CompilerParams(vmem_limit_bytes=4 << 20),
        name="pack",
    )(where, *[in_vmem(x) for x in (own_kv, got_kv, ratios, got_lr, starts, counts)])
    back1, back2 = [], []
    for j in range(CHUNKS):
        back1.append(moved(own[j], 2))
        back2.append(moved(own[j], 4))
    got_q = swapped(query[0])
    got_g = swapped(upstream[0])
    joint = pltpu.VMEM((CHIP, CHUNKS * width), BF16)
    scalars, docs, q_all, g_all = pl.pallas_call(
        partial(join_kernel, seq_len),
        out_shape=(
            jax.ShapeDtypeStruct((2 + 2 * (CHIP // SUB),), jnp.int32),
            pltpu.VMEM((8, 128), F32),
            joint,
            joint,
        ),
        in_specs=[smem, hbm, hbm] + [vmem] * 4,
        out_specs=(smem,) + (vmem,) * 3,
        scratch_shapes=[pltpu.SemaphoreType.DMA((2,))],
        compiler_params=pltpu.CompilerParams(vmem_limit_bytes=8 << 20),
        name="join",
    )(where, in_hbm(query[0]), in_hbm(upstream[0]), *[in_vmem(x) for x in (got_q, got_g, starts, counts)])
    more_docs = exchanged(docs, 1)

    dq_mine, dq_other, d_own, d_a, d_b = [], [], [], [], []
    for j in range(CHUNKS):
        operands = (q_all, g_all, own[j], back1[j], back2[j], starts, *dq_other[-1:])
        outs = pl.pallas_call(
            partial(attention_kernel, j),
            in_specs=[smem] + [vmem] * len(operands),
            input_output_aliases={len(operands): 1} if j else {},
            out_specs=[vmem] * 5,
            scratch_shapes=[
                pltpu.VMEM((WIN, DH), BF16),
                pltpu.VMEM((WIN, DH), BF16),
                pltpu.VMEM((LANES, DH), BF16),
                pltpu.VMEM((LANES, DH), BF16),
                pltpu.VMEM((SPANS[-1], LANES), F32),
                pltpu.VMEM((SPANS[-1], LANES), F32),
                pltpu.VMEM((WIN, DH), F32),
                pltpu.VMEM((WIN, DH), F32),
                pltpu.VMEM((DH, LANES), F32),
                pltpu.VMEM((SUB + CHIP, width), BF16),
            ],
            out_shape=[
                pltpu.VMEM((ROWS, width), BF16),
                pltpu.VMEM((ROWS, CHUNKS * width), BF16),
                pltpu.VMEM((CHIP, 2 * DH), F32),
                pltpu.VMEM((CHIP, 2 * DH), BF16),
                pltpu.VMEM((PACK, 2 * DH), BF16),
            ],
            compiler_params=pltpu.CompilerParams(vmem_limit_bytes=24 << 20),
        )(scalars, *[in_vmem(x) for x in operands])
        for kept, out in zip((dq_mine, dq_other, d_own, d_a, d_b), outs):
            kept.append(out)

    got_a, got_b = [], []
    for j in range(CHUNKS):
        got_a.append(moved(d_a[j], -2))
        got_b.append(moved(d_b[j], -4))
    dq_got = swapped(dq_other[-1])
    docs = docs + more_docs
    more_docs = exchanged(docs, 2)
    tails = (own[0], back1[0], back2[0], got_b[0])
    d_query, scale_mine, scale_other = pl.pallas_call(
        partial(query_kernel, seq_len),
        grid=(2 * CHUNKS,),
        out_shape=(
            jax.ShapeDtypeStruct((ROWS, HQ * DH), BF16),
            pltpu.VMEM((ROWS, DH), F32),
            pltpu.VMEM((ROWS, DH), F32),
        ),
        in_specs=[smem] + [vmem] * 11,
        out_specs=(pl.BlockSpec((ROWS, width), lambda i: (0, i)), vmem, vmem),
        compiler_params=pltpu.CompilerParams(vmem_limit_bytes=8 << 20),
        name="q_out",
    )(where, *[in_vmem(x) for x in (starts, counts, docs, more_docs, *tails, *dq_mine, dq_got)])
    half = pltpu.VMEM((ROWS, 2 * CHUNKS * DH), BF16)
    kv_mine, kv_send = pl.pallas_call(
        key_value_kernel,
        out_shape=(half, half),
        in_specs=[vmem] * 8,
        out_specs=(vmem, vmem),
        compiler_params=pltpu.CompilerParams(vmem_limit_bytes=4 << 20),
        name="kv_out",
    )(*[in_vmem(x) for x in (scale_mine, scale_other, *d_own, *got_a, *got_b)])
    kv_got = swapped(kv_send)
    cut = CHUNKS * DH
    lower, upper = (jnp.where(core == 0, kv_mine, kv_got), jnp.where(core == 0, kv_got, kv_mine))
    d_key_value = jnp.concatenate([lower[:, :cut], upper[:, :cut], lower[:, cut:], upper[:, cut:]], axis=1)
    return (d_query[None], d_key_value[None])


def solution(mesh):
    return jax.shard_map(
        local,
        mesh=mesh,
        in_specs=(
            P("dp", "ctx", None),
            P("dp", "ctx", None),
            P("dp", "ctx", None),
            P("dp", "ctx"),
            P("dp", None),
            P("dp", None),
        ),
        out_specs=(P("dp", "ctx", None), P("dp", "ctx", None)),
        check_vma=False,
    )
```

```python
from functools import partial

import jax
import jax.numpy as jnp
from jax import lax
from jax.experimental import pallas as pl
from jax.experimental.pallas import tpu as pltpu
from jax.sharding import PartitionSpec as P


HQ = 32
HK = 4
DH = 128
LOSS_SCALE = 65536
ROWS = 192
CHIP = 2 * ROWS
WIN = 3 * CHIP
GROUP = HQ // HK
SUB = 96
LANES = SUB * GROUP
SPANS = (256, 512, 640, 704, 784, 896)
CHUNKS = 2
TAIL = 16
PACK = CHIP + TAIL
MASKED = -1e30
SCALE = DH ** (-0.5)
LOG2E = 1.4426950408889634
HALVES = 1
PART = LANES // HALVES
SHARED = 384
F32 = jnp.float32
BF16 = jnp.bfloat16


def to_column(row, shift=0):
    n = row.shape[1]
    r = lax.broadcasted_iota(jnp.int32, (n, n), 0)
    c = lax.broadcasted_iota(jnp.int32, (n, n), 1)
    return jnp.sum(jnp.where(c == r + shift, row, 0), axis=1, keepdims=True)


def end_row(starts, seq_len):
    n = starts.shape[1]
    r = lax.broadcasted_iota(jnp.int32, (n, n), 0)
    c = lax.broadcasted_iota(jnp.int32, (n, n), 1)
    col = to_column(starts)
    row = jnp.sum(jnp.where(r == c + 1, col, 0), axis=0, keepdims=True)
    lane = lax.broadcasted_iota(jnp.int32, (1, n), 1)
    return jnp.where(lane == n - 1, seq_len, row)


def pack_kernel(seq_len, idx_ref, kv_ref, got_ref, lr_ref, got_lr_ref, st_ref, ct_ref, *own_refs):
    index = idx_ref[0]
    core = index % 2
    for half in range(2):

        @pl.when(core == half)
        def _():
            for j in range(CHUNKS):
                for k in range(2):
                    lo = k * HK * DH + (half * CHUNKS + j) * DH
                    own_refs[j][0:ROWS, k * DH : (k + 1) * DH] = kv_ref[:, lo : lo + DH]
                    own_refs[j][ROWS:CHIP, k * DH : (k + 1) * DH] = got_ref[:, lo : lo + DH]

    starts = st_ref[...]
    n = starts.shape[1]
    row_i = lax.broadcasted_iota(jnp.int32, (n, 1), 0)
    st = to_column(starts)
    en = jnp.where(row_i == n - 1, seq_len, to_column(starts, 1))
    first = jnp.maximum(st, en - to_column(ct_ref[...]))
    lane = lax.broadcasted_iota(jnp.int32, (n, ROWS), 1)
    part = jnp.zeros((n, 1), F32)
    for ref, where in ((lr_ref, index), (got_lr_ref, index + 1 - 2 * core)):
        pos = where * ROWS + lane
        part = part + jnp.sum(jnp.where((pos >= first) & (pos < en), ref[...], 0.0), axis=1, keepdims=True)
    r = lax.broadcasted_iota(jnp.int32, (n, n), 0)
    c = lax.broadcasted_iota(jnp.int32, (n, n), 1)
    part = jnp.sum(jnp.where(r == c, part, 0.0), axis=0, keepdims=True)
    high = part.astype(BF16).astype(F32)
    rest = part - high
    mid = rest.astype(BF16).astype(F32)
    low = rest - mid
    k = lax.broadcasted_iota(jnp.int32, (TAIL, n), 0)
    tail = jnp.where(k == 0, high, jnp.where(k == 1, mid, jnp.where(k == 2, low, 0.0))).astype(BF16)
    for ref in own_refs:
        ref[CHIP:PACK, :] = jnp.zeros((TAIL, 2 * DH), BF16)
    own_refs[0][CHIP:PACK, 0:n] = tail


def early_kernel(kv_hbm, lr_ref, st_ref, ct_ref, kv_ref, lr_out, st_out, ct_out, sem):
    copy = pltpu.make_async_copy(kv_hbm, kv_ref, sem)
    copy.start()
    lr_out[...] = lr_ref[...]
    st_out[...] = st_ref[...]
    ct_out[...] = ct_ref[...]
    copy.wait()


def halves_kernel(idx_ref, q_hbm, g_hbm, snd_ref, q_all, g_all, sems):
    core = idx_ref[0] % 2
    width = q_all.shape[1]
    rows = pl.ds(pl.multiple_of(core * ROWS, ROWS), ROWS)
    mine = pl.ds(pl.multiple_of(core * width, width), width)
    theirs = pl.ds(pl.multiple_of((1 - core) * width, width), width)
    copies = [
        pltpu.make_async_copy(q_hbm.at[:, theirs], snd_ref.at[0], sems.at[0]),
        pltpu.make_async_copy(g_hbm.at[:, theirs], snd_ref.at[1], sems.at[1]),
        pltpu.make_async_copy(q_hbm.at[:, mine], q_all.at[rows], sems.at[2]),
        pltpu.make_async_copy(g_hbm.at[:, mine], g_all.at[rows], sems.at[3]),
    ]
    for copy in copies:
        copy.start()
    for copy in copies:
        copy.wait()


def join_kernel(seq_len, idx_ref, got_ref, q_in, g_in, st_ref, ct_ref, sc_ref, cnt_ref, q_all, g_all):
    core = idx_ref[0] % 2
    mine = pl.ds(pl.multiple_of(core * ROWS, ROWS), ROWS)
    other = pl.ds(pl.multiple_of((1 - core) * ROWS, ROWS), ROWS)
    index = idx_ref[0]
    first = index // 2 * CHIP
    base = first - (WIN - CHIP)
    sc_ref[0] = index % 2
    sc_ref[1] = base
    starts = st_ref[...].astype(F32)
    for s in range(CHIP // SUB):
        at = (first + s * SUB).astype(F32)
        start = jnp.max(jnp.where(starts <= at, starts, 0.0)).astype(jnp.int32)
        low = jnp.maximum(start - base, 0) // 16 * 16
        need = (WIN - CHIP) + (s + 1) * SUB - low
        pick = jnp.int32(0)
        span = jnp.int32(SPANS[0])
        for v in range(1, len(SPANS)):
            more = need > SPANS[v - 1]
            pick = jnp.where(more, v, pick)
            span = jnp.where(more, SPANS[v], span)
        sc_ref[2 + 2 * s] = jnp.minimum(low, WIN - span)
        sc_ref[3 + 2 * s] = pick
    used = jnp.sum(jnp.where(ct_ref[...] > 0, 1.0, 0.0), axis=1, keepdims=True)
    cnt_ref[...] = jnp.broadcast_to(used, cnt_ref.shape)
    slots = st_ref[...]
    ends = end_row(slots, seq_len)
    first_answer = jnp.maximum(slots, ends - ct_ref[...])

    def answers(where):
        pos = where * ROWS + lax.broadcasted_iota(jnp.int32, (ROWS, slots.shape[1]), 0)
        hit = jnp.where((pos >= first_answer) & (pos < ends), 1.0, 0.0)
        return jnp.sum(hit, axis=1, keepdims=True) > 0.5

    q_all[other, :] = got_ref[0]
    g_all[other, :] = jnp.where(answers(index + 1 - 2 * core), got_ref[1], jnp.zeros((), BF16))
    g_all[mine, :] = jnp.where(answers(index), g_in[mine, :], jnp.zeros((), BF16))


def nt(a, b):
    return lax.dot_general(a, b, (((1,), (1,)), ((), ())), preferred_element_type=F32)


def nn(a, b):
    return lax.dot_general(a, b, (((1,), (0,)), ((), ())), preferred_element_type=F32)


def tn(a, b):
    return lax.dot_general(a, b, (((0,), (0,)), ((), ())), preferred_element_type=F32)


def fold(x, op):
    out = x[0:8]
    for i in range(8, x.shape[0], 8):
        out = op(out, x[i : i + 8])
    return out


def attention_kernel(chunk, sc_ref, q_all, g_all, own_ref, a_ref, b_ref, st_ref, *refs):
    refs = refs[1:] if chunk else refs
    dq_own_ref, dq_other_ref, d_own_ref, d_a_ref, d_b_ref, *refs = refs
    k_all, v_all, q_now, g_now, s_buf, d_buf, k_acc, v_acc, dq_now, dq_all = refs
    core = sc_ref[0]
    base = sc_ref[1]
    mine = pl.multiple_of(core * ROWS, ROWS)
    other = pl.multiple_of((1 - core) * ROWS, ROWS)
    width = GROUP * DH
    for i, src in enumerate((b_ref, a_ref, own_ref)):
        for at, lo in ((mine, 0), (other, ROWS)):
            rows = pl.ds(i * CHIP + at, ROWS)
            k_all[rows, :] = src[lo : lo + ROWS, 0:DH]
            v_all[rows, :] = src[lo : lo + ROWS, DH : 2 * DH]
    k_acc[...] = jnp.zeros(k_acc.shape, F32)
    v_acc[...] = jnp.zeros(v_acc.shape, F32)
    starts = st_ref[...]
    st_col = to_column(starts)

    def flush(row_first):
        done = dq_now[...].T
        for h in range(GROUP):
            dq_all[pl.ds(row_first, SUB), h * DH : (h + 1) * DH] = done[h * SUB : (h + 1) * SUB].astype(BF16)

    def span_step(span, key_first, row_first, low, pos):
        pieces = [(o, min(256, span - o)) for o in range(0, span, 256)]
        flush(row_first)
        state = [{} for _ in range(HALVES)]

        def rows_of(o, size):
            return pl.ds(pl.multiple_of(key_first + o, 16), size)

        def score(i, o, size):
            part = slice(i * PART, (i + 1) * PART)
            scores = nt(k_all[rows_of(o, size), :], q_now[part, :])
            key_pos = base + key_first + o + lax.broadcasted_iota(jnp.int32, (size, SHARED), 0)
            seen = (key_pos >= low) & (key_pos <= pos)
            scores = jnp.where(jnp.concatenate([seen] * (PART // SHARED), axis=1), scores, MASKED)
            s_buf[o : o + size, part] = scores
            top = fold(scores, jnp.maximum)
            state[i]["top"] = top if o == 0 else jnp.maximum(state[i]["top"], top)

        def weigh(i, o, size):
            part = slice(i * PART, (i + 1) * PART)
            if o == 0:
                state[i]["peak"] = jnp.max(state[i]["top"], axis=0, keepdims=True) * (SCALE * LOG2E)
            d_probs = nt(v_all[rows_of(o, size), :], g_now[part, :])
            weight = jnp.exp2(s_buf[o : o + size, part] * (SCALE * LOG2E) - state[i]["peak"])
            s_buf[o : o + size, part] = weight
            d_buf[o : o + size, part] = d_probs
            total = fold(weight, jnp.add)
            delta = fold(weight * d_probs, jnp.add)
            state[i]["total"] = total if o == 0 else state[i]["total"] + total
            state[i]["delta"] = delta if o == 0 else state[i]["delta"] + delta

        def finish(i, o, size):
            part = slice(i * PART, (i + 1) * PART)
            if o == 0:
                inverse = 1.0 / jnp.sum(state[i]["total"], axis=0, keepdims=True)
                state[i]["inverse"] = inverse
                state[i]["delta"] = jnp.sum(state[i]["delta"], axis=0, keepdims=True) * inverse
            rows = rows_of(o, size)
            probs = s_buf[o : o + size, part] * state[i]["inverse"]
            d_scores = (probs * (d_buf[o : o + size, part] - state[i]["delta"])).astype(BF16)
            v_acc[rows, :] += nn(probs.astype(BF16), g_now[part, :])
            k_acc[rows, :] += nn(d_scores, q_now[part, :])
            dq = tn(k_all[rows, :], d_scores)
            state[i]["dq"] = dq if o == 0 else state[i]["dq"] + dq

        stages = (score, weigh, finish)
        for t in range(len(stages) + HALVES - 1):
            for o, size in pieces:
                for i in range(HALVES):
                    if 0 <= t - i < len(stages):
                        stages[t - i](i, o, size)
        for i in range(HALVES):
            dq_now[:, i * PART : (i + 1) * PART] = state[i]["dq"] * SCALE

    def step(s, carry):
        key_first = pl.multiple_of(sc_ref[2 + 2 * s], 16)
        pick = sc_ref[3 + 2 * s]
        row_first = pl.multiple_of(s * SUB, SUB)
        for h in range(GROUP):
            col = chunk * width + h * DH
            q_now[h * SUB : (h + 1) * SUB, :] = q_all[pl.ds(row_first, SUB), col : col + DH]
            g_now[h * SUB : (h + 1) * SUB, :] = g_all[pl.ds(row_first, SUB), col : col + DH]
        lane = lax.broadcasted_iota(jnp.int32, (1, SHARED), 1)
        pos = base + (WIN - CHIP) + row_first + lane % SUB
        low = jnp.max(jnp.where(st_col <= pos, st_col, 0), axis=0, keepdims=True)
        for v, span in enumerate(SPANS):
            pl.when(pick == v)(partial(span_step, span, key_first, row_first, low, pos))
        return carry

    lax.fori_loop(0, CHIP // SUB, step, 0)
    flush(CHIP)
    dq_own_ref[...] = dq_all[pl.ds(SUB + mine, ROWS), :]
    dq_other_ref[:, chunk * width : (chunk + 1) * width] = dq_all[pl.ds(SUB + other, ROWS), :]
    for i, dst in enumerate((d_b_ref, d_a_ref, d_own_ref)):
        for at, lo in ((mine, 0), (other, ROWS)):
            rows = pl.ds(i * CHIP + at, ROWS)
            dst[lo : lo + ROWS, 0:DH] = (k_acc[rows, :] * SCALE).astype(dst.dtype)
            dst[lo : lo + ROWS, DH : 2 * DH] = v_acc[rows, :].astype(dst.dtype)
    d_b_ref[CHIP:PACK, 0:DH] = own_ref[CHIP:PACK, 0:DH]
    d_b_ref[CHIP:PACK, DH : 2 * DH] = a_ref[CHIP:PACK, 0:DH]


def row_coefs(starts, ends, coef, first):
    n = starts.shape[1]
    pos = first + lax.broadcasted_iota(jnp.int32, (ROWS, n), 0)
    return jnp.sum(jnp.where((pos >= starts) & (pos < ends), coef, 0.0), axis=1, keepdims=True)


def query_kernel(seq_len, idx_ref, st_ref, ct_ref, docs_ref, more_ref, *refs):
    tail_refs, mine_refs, got_ref = refs[0:4], refs[4:6], refs[6]
    out_ref, scale_ref, other_ref = refs[7:10]
    index = idx_ref[0]
    step = pl.program_id(0)

    @pl.when(step == 0)
    def _():
        starts = st_ref[...]
        n = starts.shape[1]
        sums = jnp.zeros((1, n), F32)
        for ref in tail_refs:
            sums = sums + jnp.sum(ref[CHIP:PACK, 0:n].astype(F32), axis=0, keepdims=True)
        sums = sums + jnp.sum(tail_refs[-1][CHIP:PACK, DH : DH + n].astype(F32), axis=0, keepdims=True)
        size = jnp.maximum(ct_ref[...], 1).astype(F32)
        coef = LOSS_SCALE * 2.0 / (1.0 + jnp.exp(-sums / size)) / (size * (docs_ref[0:1, 0:n] + more_ref[0:1, 0:n]))
        ends = end_row(starts, seq_len)
        for dst, where in ((scale_ref, index), (other_ref, index // 2 * 2 + 1 - index % 2)):
            dst[...] = jnp.broadcast_to(row_coefs(starts, ends, coef, where * ROWS), dst.shape)

    scale = scale_ref[:, 0:1]
    width = GROUP * DH
    for k in range(2):
        for j in range(CHUNKS):

            @pl.when(step == (index % 2 + k) % 2 * CHUNKS + j)
            def _():
                src = got_ref[:, j * width : (j + 1) * width] if k else mine_refs[j][...]
                out_ref[...] = (src.astype(F32) * scale).astype(BF16)


def key_value_kernel(*refs):
    scale_refs, own_refs, a_refs, b_refs, outs = refs[0:2], refs[2:4], refs[4:6], refs[6:8], refs[8:10]
    for i in range(2):
        rows = slice(i * ROWS, (i + 1) * ROWS)
        scale = scale_refs[i][...]
        for j in range(CHUNKS):
            for k in range(2):
                cols = slice(k * DH, (k + 1) * DH)
                out = own_refs[j][rows, cols] + a_refs[j][rows, cols].astype(F32) + b_refs[j][rows, cols].astype(F32)
                at = (k * CHUNKS + j) * DH
                outs[i][:, at : at + DH] = (out * scale).astype(BF16)


def in_vmem(x):
    return pltpu.with_memory_space_constraint(x, pltpu.VMEM)


def in_hbm(x):
    return pltpu.with_memory_space_constraint(x, pltpu.HBM)


def local(query, key_value, upstream, log_ratio, doc_starts, answer_counts):
    count = lax.axis_size("ctx")
    seq_len = ROWS * count
    index = lax.axis_index("ctx").astype(jnp.int32)
    core = index % 2
    where = index.reshape(1)
    smem = pl.BlockSpec(memory_space=pltpu.SMEM)
    vmem = pl.BlockSpec(memory_space=pltpu.VMEM)

    def moved(value, steps):
        return lax.ppermute(value, "ctx", [(i, (i + steps) % count) for i in range(count)])

    def moved_two_chips(value, steps):
        pairs = [(i, i + steps) for i in range(count) if 0 <= i + steps < count]
        senders, receivers = sorted(set(range(count)) - {i for i, _ in pairs}), sorted(set(range(count)) - {i for _, i in pairs})
        half = len(senders) // 2
        return lax.ppermute(value, "ctx", pairs + list(zip(senders, receivers[half:] + receivers[:half])))

    def swapped(value):
        return lax.ppermute(value, "ctx", [(i, i ^ 1) for i in range(count)])

    def exchanged(value, bit):
        return lax.ppermute(value, "dp", [(i, i ^ bit) for i in range(lax.axis_size("dp"))])

    width = GROUP * DH
    got_lr = swapped(log_ratio)
    got_kv = swapped(key_value[0])
    hbm = pl.BlockSpec(memory_space=pl.ANY)
    slots = doc_starts.shape[1]
    own_kv, ratios, starts, counts = pl.pallas_call(
        early_kernel,
        out_shape=(
            pltpu.VMEM((ROWS, 2 * HK * DH), BF16),
            pltpu.VMEM((1, ROWS), F32),
            pltpu.VMEM((1, slots), jnp.int32),
            pltpu.VMEM((1, slots), jnp.int32),
        ),
        in_specs=[hbm] + [vmem] * 3,
        out_specs=(vmem,) * 4,
        scratch_shapes=[pltpu.SemaphoreType.DMA],
        compiler_params=pltpu.CompilerParams(vmem_limit_bytes=4 << 20),
        name="early",
    )(*[in_hbm(x) for x in (key_value[0], log_ratio, doc_starts, answer_counts)])
    packed = pltpu.VMEM((PACK, 2 * DH), BF16)
    own = pl.pallas_call(
        partial(pack_kernel, seq_len),
        out_shape=(packed,) * CHUNKS,
        in_specs=[smem] + [vmem] * 6,
        out_specs=(vmem,) * CHUNKS,
        compiler_params=pltpu.CompilerParams(vmem_limit_bytes=4 << 20),
        name="pack",
    )(where, *[in_vmem(x) for x in (own_kv, got_kv, ratios, got_lr, starts, counts)])
    back1, back2 = [], []
    for j in range(CHUNKS):
        back1.append(moved(own[j], 2))
        back2.append(moved_two_chips(own[j], 4))
    joint = pltpu.VMEM((CHIP, CHUNKS * width), BF16)
    to_send, q_mine, g_mine = pl.pallas_call(
        halves_kernel,
        out_shape=(pltpu.VMEM((2, ROWS, CHUNKS * width), BF16), joint, joint),
        in_specs=[smem, hbm, hbm],
        out_specs=(vmem,) * 3,
        scratch_shapes=[pltpu.SemaphoreType.DMA((4,))],
        compiler_params=pltpu.CompilerParams(vmem_limit_bytes=8 << 20),
        name="halves",
    )(where, in_hbm(query[0]), in_hbm(upstream[0]))
    got_rows = swapped(to_send)
    scalars, docs, q_all, g_all = pl.pallas_call(
        partial(join_kernel, seq_len),
        out_shape=(
            jax.ShapeDtypeStruct((2 + 2 * (CHIP // SUB),), jnp.int32),
            pltpu.VMEM((8, 128), F32),
            joint,
            joint,
        ),
        in_specs=[smem] + [vmem] * 5,
        out_specs=(smem,) + (vmem,) * 3,
        input_output_aliases={2: 2, 3: 3},
        compiler_params=pltpu.CompilerParams(vmem_limit_bytes=8 << 20),
        name="join",
    )(where, *[in_vmem(x) for x in (got_rows, q_mine, g_mine, starts, counts)])
    more_docs = exchanged(docs, 1)

    dq_mine, dq_other, d_own, d_a, d_b = [], [], [], [], []
    for j in range(CHUNKS):
        operands = (q_all, g_all, own[j], back1[j], back2[j], starts, *dq_other[-1:])
        outs = pl.pallas_call(
            partial(attention_kernel, j),
            in_specs=[smem] + [vmem] * len(operands),
            input_output_aliases={len(operands): 1} if j else {},
            out_specs=[vmem] * 5,
            scratch_shapes=[
                pltpu.VMEM((WIN, DH), BF16),
                pltpu.VMEM((WIN, DH), BF16),
                pltpu.VMEM((LANES, DH), BF16),
                pltpu.VMEM((LANES, DH), BF16),
                pltpu.VMEM((SPANS[-1], LANES), F32),
                pltpu.VMEM((SPANS[-1], LANES), F32),
                pltpu.VMEM((WIN, DH), F32),
                pltpu.VMEM((WIN, DH), F32),
                pltpu.VMEM((DH, LANES), F32),
                pltpu.VMEM((SUB + CHIP, width), BF16),
            ],
            out_shape=[
                pltpu.VMEM((ROWS, width), BF16),
                pltpu.VMEM((ROWS, CHUNKS * width), BF16),
                pltpu.VMEM((CHIP, 2 * DH), F32),
                pltpu.VMEM((CHIP, 2 * DH), BF16),
                pltpu.VMEM((PACK, 2 * DH), BF16),
            ],
            compiler_params=pltpu.CompilerParams(vmem_limit_bytes=24 << 20),
        )(scalars, *[in_vmem(x) for x in operands])
        for kept, out in zip((dq_mine, dq_other, d_own, d_a, d_b), outs):
            kept.append(out)

    got_a, got_b = [], []
    for j in range(CHUNKS):
        got_a.append(moved(d_a[j], -2))
        got_b.append((moved_two_chips if j else moved)(d_b[j], -4))
    dq_got = swapped(dq_other[-1])
    docs = docs + more_docs
    more_docs = exchanged(docs, 2)
    tails = (own[0], back1[0], back2[0], got_b[0])
    d_query, scale_mine, scale_other = pl.pallas_call(
        partial(query_kernel, seq_len),
        grid=(2 * CHUNKS,),
        out_shape=(
            jax.ShapeDtypeStruct((ROWS, HQ * DH), BF16),
            pltpu.VMEM((ROWS, DH), F32),
            pltpu.VMEM((ROWS, DH), F32),
        ),
        in_specs=[smem] + [vmem] * 11,
        out_specs=(pl.BlockSpec((ROWS, width), lambda i: (0, i)), vmem, vmem),
        compiler_params=pltpu.CompilerParams(vmem_limit_bytes=8 << 20),
        name="q_out",
    )(where, *[in_vmem(x) for x in (starts, counts, docs, more_docs, *tails, *dq_mine, dq_got)])
    half = pltpu.VMEM((ROWS, 2 * CHUNKS * DH), BF16)
    kv_mine, kv_send = pl.pallas_call(
        key_value_kernel,
        out_shape=(half, half),
        in_specs=[vmem] * 8,
        out_specs=(vmem, vmem),
        compiler_params=pltpu.CompilerParams(vmem_limit_bytes=4 << 20),
        name="kv_out",
    )(*[in_vmem(x) for x in (scale_mine, scale_other, *d_own, *got_a, *got_b)])
    kv_got = swapped(kv_send)
    cut = CHUNKS * DH
    lower, upper = (jnp.where(core == 0, kv_mine, kv_got), jnp.where(core == 0, kv_got, kv_mine))
    d_key_value = jnp.concatenate([lower[:, :cut], upper[:, :cut], lower[:, cut:], upper[:, cut:]], axis=1)
    return (d_query[None], d_key_value[None])


def solution(mesh):
    return jax.shard_map(
        local,
        mesh=mesh,
        in_specs=(
            P("dp", "ctx", None),
            P("dp", "ctx", None),
            P("dp", "ctx", None),
            P("dp", "ctx"),
            P("dp", None),
            P("dp", None),
        ),
        out_specs=(P("dp", "ctx", None), P("dp", "ctx", None)),
        check_vma=False,
    )
```

```python
from functools import partial

import jax
import jax.numpy as jnp
from jax import lax
from jax.experimental import pallas as pl
from jax.experimental.pallas import tpu as pltpu
from jax.sharding import PartitionSpec as P


HQ = 32
HK = 4
DH = 128
LOSS_SCALE = 65536
ROWS = 192
CHIP = 2 * ROWS
WIN = 3 * CHIP
GROUP = HQ // HK
SUB = 96
LANES = SUB * GROUP
SPANS = (256, 512, 640, 704, 784, 896)
CHUNKS = 2
TAIL = 16
PACK = CHIP + TAIL
MASKED = -1e30
SCALE = DH ** (-0.5)
LOG2E = 1.4426950408889634
HALVES = 1
PART = LANES // HALVES
SHARED = 384
F32 = jnp.float32
BF16 = jnp.bfloat16


def to_column(row, shift=0):
    n = row.shape[1]
    r = lax.broadcasted_iota(jnp.int32, (n, n), 0)
    c = lax.broadcasted_iota(jnp.int32, (n, n), 1)
    return jnp.sum(jnp.where(c == r + shift, row, 0), axis=1, keepdims=True)


def end_row(starts, seq_len):
    n = starts.shape[1]
    r = lax.broadcasted_iota(jnp.int32, (n, n), 0)
    c = lax.broadcasted_iota(jnp.int32, (n, n), 1)
    col = to_column(starts)
    row = jnp.sum(jnp.where(r == c + 1, col, 0), axis=0, keepdims=True)
    lane = lax.broadcasted_iota(jnp.int32, (1, n), 1)
    return jnp.where(lane == n - 1, seq_len, row)


def pack_kernel(seq_len, idx_ref, kv_ref, got_ref, lr_ref, got_lr_ref, st_ref, ct_ref, *own_refs):
    index = idx_ref[0]
    core = index % 2
    for half in range(2):

        @pl.when(core == half)
        def _():
            for j in range(CHUNKS):
                for k in range(2):
                    lo = k * HK * DH + (half * CHUNKS + j) * DH
                    own_refs[j][0:ROWS, k * DH : (k + 1) * DH] = kv_ref[:, lo : lo + DH]
                    own_refs[j][ROWS:CHIP, k * DH : (k + 1) * DH] = got_ref[:, lo : lo + DH]

    starts = st_ref[...]
    n = starts.shape[1]
    row_i = lax.broadcasted_iota(jnp.int32, (n, 1), 0)
    st = to_column(starts)
    en = jnp.where(row_i == n - 1, seq_len, to_column(starts, 1))
    first = jnp.maximum(st, en - to_column(ct_ref[...]))
    lane = lax.broadcasted_iota(jnp.int32, (n, ROWS), 1)
    part = jnp.zeros((n, 1), F32)
    for ref, where in ((lr_ref, index), (got_lr_ref, index + 1 - 2 * core)):
        pos = where * ROWS + lane
        part = part + jnp.sum(jnp.where((pos >= first) & (pos < en), ref[...], 0.0), axis=1, keepdims=True)
    r = lax.broadcasted_iota(jnp.int32, (n, n), 0)
    c = lax.broadcasted_iota(jnp.int32, (n, n), 1)
    part = jnp.sum(jnp.where(r == c, part, 0.0), axis=0, keepdims=True)
    high = part.astype(BF16).astype(F32)
    rest = part - high
    mid = rest.astype(BF16).astype(F32)
    low = rest - mid
    k = lax.broadcasted_iota(jnp.int32, (TAIL, n), 0)
    tail = jnp.where(k == 0, high, jnp.where(k == 1, mid, jnp.where(k == 2, low, 0.0))).astype(BF16)
    for ref in own_refs:
        ref[CHIP:PACK, :] = jnp.zeros((TAIL, 2 * DH), BF16)
    own_refs[0][CHIP:PACK, 0:n] = tail


def early_kernel(kv_hbm, lr_ref, st_ref, ct_ref, kv_ref, lr_out, st_out, ct_out, sem):
    copy = pltpu.make_async_copy(kv_hbm, kv_ref, sem)
    copy.start()
    lr_out[...] = lr_ref[...]
    st_out[...] = st_ref[...]
    ct_out[...] = ct_ref[...]
    copy.wait()


def halves_kernel(idx_ref, q_hbm, g_hbm, snd_ref, q_all, g_all, sems):
    core = idx_ref[0] % 2
    width = q_all.shape[1]
    rows = pl.ds(pl.multiple_of(core * ROWS, ROWS), ROWS)
    mine = pl.ds(pl.multiple_of(core * width, width), width)
    theirs = pl.ds(pl.multiple_of((1 - core) * width, width), width)
    copies = [
        pltpu.make_async_copy(q_hbm.at[:, theirs], snd_ref.at[0], sems.at[0]),
        pltpu.make_async_copy(g_hbm.at[:, theirs], snd_ref.at[1], sems.at[1]),
        pltpu.make_async_copy(q_hbm.at[:, mine], q_all.at[rows], sems.at[2]),
        pltpu.make_async_copy(g_hbm.at[:, mine], g_all.at[rows], sems.at[3]),
    ]
    for copy in copies:
        copy.start()
    for copy in copies:
        copy.wait()


def join_kernel(seq_len, idx_ref, got_ref, q_in, g_in, st_ref, ct_ref, sc_ref, cnt_ref, q_all, g_all):
    core = idx_ref[0] % 2
    mine = pl.ds(pl.multiple_of(core * ROWS, ROWS), ROWS)
    other = pl.ds(pl.multiple_of((1 - core) * ROWS, ROWS), ROWS)
    index = idx_ref[0]
    first = index // 2 * CHIP
    base = first - (WIN - CHIP)
    sc_ref[0] = index % 2
    sc_ref[1] = base
    starts = st_ref[...].astype(F32)
    for s in range(CHIP // SUB):
        at = (first + s * SUB).astype(F32)
        start = jnp.max(jnp.where(starts <= at, starts, 0.0)).astype(jnp.int32)
        low = jnp.maximum(start - base, 0) // 16 * 16
        need = (WIN - CHIP) + (s + 1) * SUB - low
        pick = jnp.int32(0)
        span = jnp.int32(SPANS[0])
        for v in range(1, len(SPANS)):
            more = need > SPANS[v - 1]
            pick = jnp.where(more, v, pick)
            span = jnp.where(more, SPANS[v], span)
        sc_ref[2 + 2 * s] = jnp.minimum(low, WIN - span)
        sc_ref[3 + 2 * s] = pick
    used = jnp.sum(jnp.where(ct_ref[...] > 0, 1.0, 0.0), axis=1, keepdims=True)
    cnt_ref[...] = jnp.broadcast_to(used, cnt_ref.shape)
    slots = st_ref[...]
    ends = end_row(slots, seq_len)
    first_answer = jnp.maximum(slots, ends - ct_ref[...])

    def answers(where):
        pos = where * ROWS + lax.broadcasted_iota(jnp.int32, (ROWS, slots.shape[1]), 0)
        hit = jnp.where((pos >= first_answer) & (pos < ends), 1.0, 0.0)
        return jnp.sum(hit, axis=1, keepdims=True) > 0.5

    q_all[other, :] = got_ref[0]
    g_all[other, :] = jnp.where(answers(index + 1 - 2 * core), got_ref[1], jnp.zeros((), BF16))
    g_all[mine, :] = jnp.where(answers(index), g_in[mine, :], jnp.zeros((), BF16))


def nt(a, b):
    return lax.dot_general(a, b, (((1,), (1,)), ((), ())), preferred_element_type=F32)


def nn(a, b):
    return lax.dot_general(a, b, (((1,), (0,)), ((), ())), preferred_element_type=F32)


def tn(a, b):
    return lax.dot_general(a, b, (((0,), (0,)), ((), ())), preferred_element_type=F32)


def fold(x, op):
    out = x[0:8]
    for i in range(8, x.shape[0], 8):
        out = op(out, x[i : i + 8])
    return out


def attention_kernel(chunk, sc_ref, q_all, g_all, own_ref, a_ref, b_ref, st_ref, *refs):
    refs = refs[1:] if chunk else refs
    dq_own_ref, dq_other_ref, d_own_ref, d_a_ref, d_b_ref, *refs = refs
    k_all, v_all, q_now, g_now, s_buf, d_buf, k_acc, v_acc, dq_now, dq_all = refs
    core = sc_ref[0]
    base = sc_ref[1]
    mine = pl.multiple_of(core * ROWS, ROWS)
    other = pl.multiple_of((1 - core) * ROWS, ROWS)
    width = GROUP * DH
    for i, src in enumerate((b_ref, a_ref, own_ref)):
        for at, lo in ((mine, 0), (other, ROWS)):
            rows = pl.ds(i * CHIP + at, ROWS)
            k_all[rows, :] = src[lo : lo + ROWS, 0:DH]
            v_all[rows, :] = src[lo : lo + ROWS, DH : 2 * DH]
    k_acc[...] = jnp.zeros(k_acc.shape, F32)
    v_acc[...] = jnp.zeros(v_acc.shape, F32)
    starts = st_ref[...]
    st_col = to_column(starts)

    def flush(row_first):
        done = dq_now[...].T
        for h in range(GROUP):
            dq_all[pl.ds(row_first, SUB), h * DH : (h + 1) * DH] = done[h * SUB : (h + 1) * SUB].astype(BF16)

    def span_step(span, key_first, row_first, low, pos):
        pieces = [(o, min(256, span - o)) for o in range(0, span, 256)]
        flush(row_first)
        state = [{} for _ in range(HALVES)]

        def rows_of(o, size):
            return pl.ds(pl.multiple_of(key_first + o, 16), size)

        def score(i, o, size):
            part = slice(i * PART, (i + 1) * PART)
            scores = nt(k_all[rows_of(o, size), :], q_now[part, :])
            key_pos = base + key_first + o + lax.broadcasted_iota(jnp.int32, (size, SHARED), 0)
            seen = (key_pos >= low) & (key_pos <= pos)
            scores = jnp.where(jnp.concatenate([seen] * (PART // SHARED), axis=1), scores, MASKED)
            s_buf[o : o + size, part] = scores
            top = fold(scores, jnp.maximum)
            state[i]["top"] = top if o == 0 else jnp.maximum(state[i]["top"], top)

        def weigh(i, o, size):
            part = slice(i * PART, (i + 1) * PART)
            if o == 0:
                state[i]["peak"] = jnp.max(state[i]["top"], axis=0, keepdims=True) * (SCALE * LOG2E)
            d_probs = nt(v_all[rows_of(o, size), :], g_now[part, :])
            weight = jnp.exp2(s_buf[o : o + size, part] * (SCALE * LOG2E) - state[i]["peak"])
            s_buf[o : o + size, part] = weight
            d_buf[o : o + size, part] = d_probs
            total = fold(weight, jnp.add)
            delta = fold(weight * d_probs, jnp.add)
            state[i]["total"] = total if o == 0 else state[i]["total"] + total
            state[i]["delta"] = delta if o == 0 else state[i]["delta"] + delta

        def finish(i, o, size):
            part = slice(i * PART, (i + 1) * PART)
            if o == 0:
                inverse = 1.0 / jnp.sum(state[i]["total"], axis=0, keepdims=True)
                state[i]["inverse"] = inverse
                state[i]["delta"] = jnp.sum(state[i]["delta"], axis=0, keepdims=True) * inverse
            rows = rows_of(o, size)
            probs = s_buf[o : o + size, part] * state[i]["inverse"]
            d_scores = (probs * (d_buf[o : o + size, part] - state[i]["delta"])).astype(BF16)
            v_acc[rows, :] += nn(probs.astype(BF16), g_now[part, :])
            k_acc[rows, :] += nn(d_scores, q_now[part, :])
            dq = tn(k_all[rows, :], d_scores)
            state[i]["dq"] = dq if o == 0 else state[i]["dq"] + dq

        stages = (score, weigh, finish)
        for t in range(len(stages) + HALVES - 1):
            for o, size in pieces:
                for i in range(HALVES):
                    if 0 <= t - i < len(stages):
                        stages[t - i](i, o, size)
        for i in range(HALVES):
            dq_now[:, i * PART : (i + 1) * PART] = state[i]["dq"] * SCALE

    def step(s, carry):
        key_first = pl.multiple_of(sc_ref[2 + 2 * s], 16)
        pick = sc_ref[3 + 2 * s]
        row_first = pl.multiple_of(s * SUB, SUB)
        for h in range(GROUP):
            col = chunk * width + h * DH
            q_now[h * SUB : (h + 1) * SUB, :] = q_all[pl.ds(row_first, SUB), col : col + DH]
            g_now[h * SUB : (h + 1) * SUB, :] = g_all[pl.ds(row_first, SUB), col : col + DH]
        lane = lax.broadcasted_iota(jnp.int32, (1, SHARED), 1)
        pos = base + (WIN - CHIP) + row_first + lane % SUB
        low = jnp.max(jnp.where(st_col <= pos, st_col, 0), axis=0, keepdims=True)
        for v, span in enumerate(SPANS):
            pl.when(pick == v)(partial(span_step, span, key_first, row_first, low, pos))
        return carry

    lax.fori_loop(0, CHIP // SUB, step, 0)
    flush(CHIP)
    dq_own_ref[...] = dq_all[pl.ds(SUB + mine, ROWS), :]
    dq_other_ref[:, chunk * width : (chunk + 1) * width] = dq_all[pl.ds(SUB + other, ROWS), :]
    for i, dst in enumerate((d_b_ref, d_a_ref, d_own_ref)):
        for at, lo in ((mine, 0), (other, ROWS)):
            rows = pl.ds(i * CHIP + at, ROWS)
            dst[lo : lo + ROWS, 0:DH] = (k_acc[rows, :] * SCALE).astype(dst.dtype)
            dst[lo : lo + ROWS, DH : 2 * DH] = v_acc[rows, :].astype(dst.dtype)
    d_b_ref[CHIP:PACK, 0:DH] = own_ref[CHIP:PACK, 0:DH]
    d_b_ref[CHIP:PACK, DH : 2 * DH] = a_ref[CHIP:PACK, 0:DH]


def row_coefs(starts, ends, coef, first):
    n = starts.shape[1]
    pos = first + lax.broadcasted_iota(jnp.int32, (ROWS, n), 0)
    return jnp.sum(jnp.where((pos >= starts) & (pos < ends), coef, 0.0), axis=1, keepdims=True)


def query_kernel(idx_ref, scale_ref, *refs):
    mine_refs, got_ref, out_hbm, done, sems = refs[0:2], *refs[2:6]
    scale = scale_ref[:, 0:1]
    width = GROUP * DH
    copies = []
    for k in range(2):
        for j in range(CHUNKS):
            src = got_ref[:, j * width : (j + 1) * width] if k else mine_refs[j][...]
            slot = k * CHUNKS + j
            done[slot] = (src.astype(F32) * scale).astype(BF16)
            at = pl.multiple_of(((idx_ref[0] + k) % 2 * CHUNKS + j) * width, width)
            copies.append(pltpu.make_async_copy(done.at[slot], out_hbm.at[:, pl.ds(at, width)], sems.at[slot]))
            copies[-1].start()
    for copy in copies:
        copy.wait()


def place_kernel(idx_ref, mine_ref, got_ref, out_hbm, sems):
    cut = CHUNKS * DH
    copies = []
    for k, src in enumerate((mine_ref, got_ref)):
        for j in range(2):
            at = pl.multiple_of(j * HK * DH + (idx_ref[0] + k) % 2 * cut, cut)
            copies.append(
                pltpu.make_async_copy(
                    src.at[:, j * cut : (j + 1) * cut], out_hbm.at[:, pl.ds(at, cut)], sems.at[2 * k + j]
                )
            )
            copies[-1].start()
    for copy in copies:
        copy.wait()


def key_value_kernel(seq_len, idx_ref, st_ref, ct_ref, docs_ref, more_ref, *refs):
    tail_refs, own_refs, a_refs, b_refs = refs[0:3], refs[3:5], refs[5:7], refs[7:9]
    outs, scale_ref = refs[9:11], refs[11]
    index = idx_ref[0]
    starts = st_ref[...]
    n = starts.shape[1]
    sums = jnp.zeros((1, n), F32)
    for ref in (*tail_refs, b_refs[0]):
        sums = sums + jnp.sum(ref[CHIP:PACK, 0:n].astype(F32), axis=0, keepdims=True)
    sums = sums + jnp.sum(b_refs[0][CHIP:PACK, DH : DH + n].astype(F32), axis=0, keepdims=True)
    size = jnp.maximum(ct_ref[...], 1).astype(F32)
    docs = docs_ref[0:1, 0:n] + more_ref[0:1, 0:n]
    coef = LOSS_SCALE * 2.0 / (1.0 + jnp.exp(-sums / size)) / (size * docs)
    ends = end_row(starts, seq_len)
    for i, where in enumerate((index, index // 2 * 2 + 1 - index % 2)):
        rows = slice(i * ROWS, (i + 1) * ROWS)
        scale = jnp.broadcast_to(row_coefs(starts, ends, coef, where * ROWS), (ROWS, DH))
        if i == 0:
            scale_ref[...] = scale
        for j in range(CHUNKS):
            for k in range(2):
                cols = slice(k * DH, (k + 1) * DH)
                out = own_refs[j][rows, cols] + a_refs[j][rows, cols].astype(F32) + b_refs[j][rows, cols].astype(F32)
                at = (k * CHUNKS + j) * DH
                outs[i][:, at : at + DH] = (out * scale).astype(BF16)


def in_vmem(x):
    return pltpu.with_memory_space_constraint(x, pltpu.VMEM)


def in_hbm(x):
    return pltpu.with_memory_space_constraint(x, pltpu.HBM)


def local(query, key_value, upstream, log_ratio, doc_starts, answer_counts):
    count = lax.axis_size("ctx")
    seq_len = ROWS * count
    index = lax.axis_index("ctx").astype(jnp.int32)
    where = index.reshape(1)
    smem = pl.BlockSpec(memory_space=pltpu.SMEM)
    vmem = pl.BlockSpec(memory_space=pltpu.VMEM)

    def moved(value, steps):
        return lax.ppermute(value, "ctx", [(i, (i + steps) % count) for i in range(count)])

    def moved_two_chips(value, steps):
        pairs = [(i, i + steps) for i in range(count) if 0 <= i + steps < count]
        senders, receivers = sorted(set(range(count)) - {i for i, _ in pairs}), sorted(set(range(count)) - {i for _, i in pairs})
        half = len(senders) // 2
        return lax.ppermute(value, "ctx", pairs + list(zip(senders, receivers[half:] + receivers[:half])))

    def swapped(value):
        return lax.ppermute(value, "ctx", [(i, i ^ 1) for i in range(count)])

    def exchanged(value, bit):
        return lax.ppermute(value, "dp", [(i, i ^ bit) for i in range(lax.axis_size("dp"))])

    width = GROUP * DH
    got_lr = swapped(log_ratio)
    got_kv = swapped(key_value[0])
    hbm = pl.BlockSpec(memory_space=pl.ANY)
    slots = doc_starts.shape[1]
    own_kv, ratios, starts, counts = pl.pallas_call(
        early_kernel,
        out_shape=(
            pltpu.VMEM((ROWS, 2 * HK * DH), BF16),
            pltpu.VMEM((1, ROWS), F32),
            pltpu.VMEM((1, slots), jnp.int32),
            pltpu.VMEM((1, slots), jnp.int32),
        ),
        in_specs=[hbm] + [vmem] * 3,
        out_specs=(vmem,) * 4,
        scratch_shapes=[pltpu.SemaphoreType.DMA],
        compiler_params=pltpu.CompilerParams(vmem_limit_bytes=4 << 20),
        name="early",
    )(*[in_hbm(x) for x in (key_value[0], log_ratio, doc_starts, answer_counts)])
    packed = pltpu.VMEM((PACK, 2 * DH), BF16)
    own = pl.pallas_call(
        partial(pack_kernel, seq_len),
        out_shape=(packed,) * CHUNKS,
        in_specs=[smem] + [vmem] * 6,
        out_specs=(vmem,) * CHUNKS,
        compiler_params=pltpu.CompilerParams(vmem_limit_bytes=4 << 20),
        name="pack",
    )(where, *[in_vmem(x) for x in (own_kv, got_kv, ratios, got_lr, starts, counts)])
    back1, back2 = [], []
    for j in range(CHUNKS):
        back1.append(moved(own[j], 2))
        back2.append(moved_two_chips(own[j], 4))
    joint = pltpu.VMEM((CHIP, CHUNKS * width), BF16)
    to_send, q_mine, g_mine = pl.pallas_call(
        halves_kernel,
        out_shape=(pltpu.VMEM((2, ROWS, CHUNKS * width), BF16), joint, joint),
        in_specs=[smem, hbm, hbm],
        out_specs=(vmem,) * 3,
        scratch_shapes=[pltpu.SemaphoreType.DMA((4,))],
        compiler_params=pltpu.CompilerParams(vmem_limit_bytes=8 << 20),
        name="halves",
    )(where, in_hbm(query[0]), in_hbm(upstream[0]))
    got_rows = swapped(to_send)
    scalars, docs, q_all, g_all = pl.pallas_call(
        partial(join_kernel, seq_len),
        out_shape=(
            jax.ShapeDtypeStruct((2 + 2 * (CHIP // SUB),), jnp.int32),
            pltpu.VMEM((8, 128), F32),
            joint,
            joint,
        ),
        in_specs=[smem] + [vmem] * 5,
        out_specs=(smem,) + (vmem,) * 3,
        input_output_aliases={2: 2, 3: 3},
        compiler_params=pltpu.CompilerParams(vmem_limit_bytes=8 << 20),
        name="join",
    )(where, *[in_vmem(x) for x in (got_rows, q_mine, g_mine, starts, counts)])
    more_docs = exchanged(docs, 1)

    dq_mine, dq_other, d_own, d_a, d_b = [], [], [], [], []
    for j in range(CHUNKS):
        operands = (q_all, g_all, own[j], back1[j], back2[j], starts, *dq_other[-1:])
        outs = pl.pallas_call(
            partial(attention_kernel, j),
            in_specs=[smem] + [vmem] * len(operands),
            input_output_aliases={len(operands): 1} if j else {},
            out_specs=[vmem] * 5,
            scratch_shapes=[
                pltpu.VMEM((WIN, DH), BF16),
                pltpu.VMEM((WIN, DH), BF16),
                pltpu.VMEM((LANES, DH), BF16),
                pltpu.VMEM((LANES, DH), BF16),
                pltpu.VMEM((SPANS[-1], LANES), F32),
                pltpu.VMEM((SPANS[-1], LANES), F32),
                pltpu.VMEM((WIN, DH), F32),
                pltpu.VMEM((WIN, DH), F32),
                pltpu.VMEM((DH, LANES), F32),
                pltpu.VMEM((SUB + CHIP, width), BF16),
            ],
            out_shape=[
                pltpu.VMEM((ROWS, width), BF16),
                pltpu.VMEM((ROWS, CHUNKS * width), BF16),
                pltpu.VMEM((CHIP, 2 * DH), F32),
                pltpu.VMEM((CHIP, 2 * DH), BF16),
                pltpu.VMEM((PACK, 2 * DH), BF16),
            ],
            compiler_params=pltpu.CompilerParams(vmem_limit_bytes=24 << 20),
        )(scalars, *[in_vmem(x) for x in operands])
        for kept, out in zip((dq_mine, dq_other, d_own, d_a, d_b), outs):
            kept.append(out)

    got_a, got_b = [], []
    for j in range(CHUNKS):
        got_a.append(moved(d_a[j], -2))
        got_b.append((moved_two_chips if j else moved)(d_b[j], -4))
    dq_got = swapped(dq_other[-1])
    docs = docs + more_docs
    more_docs = exchanged(docs, 2)
    half = pltpu.VMEM((ROWS, 2 * CHUNKS * DH), BF16)
    operands = (starts, counts, docs, more_docs, own[0], back1[0], back2[0], *d_own, *got_a, *got_b)
    kv_mine, kv_send, scale = pl.pallas_call(
        partial(key_value_kernel, seq_len),
        out_shape=(half, half, pltpu.VMEM((ROWS, DH), F32)),
        in_specs=[smem] + [vmem] * len(operands),
        out_specs=(vmem,) * 3,
        compiler_params=pltpu.CompilerParams(vmem_limit_bytes=8 << 20),
        name="kv_out",
    )(where, *[in_vmem(x) for x in operands])
    kv_got = swapped(kv_send)
    d_query = pl.pallas_call(
        query_kernel,
        out_shape=jax.ShapeDtypeStruct((ROWS, HQ * DH), BF16),
        in_specs=[smem] + [vmem] * 4,
        out_specs=hbm,
        scratch_shapes=[pltpu.VMEM((2 * CHUNKS, ROWS, width), BF16), pltpu.SemaphoreType.DMA((2 * CHUNKS,))],
        compiler_params=pltpu.CompilerParams(vmem_limit_bytes=8 << 20),
        name="q_out",
    )(where, *[in_vmem(x) for x in (scale, *dq_mine, dq_got)])
    d_key_value = pl.pallas_call(
        place_kernel,
        out_shape=jax.ShapeDtypeStruct((ROWS, 2 * HK * DH), BF16),
        in_specs=[smem, vmem, vmem],
        out_specs=hbm,
        scratch_shapes=[pltpu.SemaphoreType.DMA((4,))],
        name="place",
    )(where, in_vmem(kv_mine), in_vmem(kv_got))
    return (d_query[None], d_key_value[None])


def solution(mesh):
    return jax.shard_map(
        local,
        mesh=mesh,
        in_specs=(
            P("dp", "ctx", None),
            P("dp", "ctx", None),
            P("dp", "ctx", None),
            P("dp", "ctx"),
            P("dp", None),
            P("dp", None),
        ),
        out_specs=(P("dp", "ctx", None), P("dp", "ctx", None)),
        check_vma=False,
    )
```

```python
from functools import partial

import jax
import jax.numpy as jnp
from jax import lax
from jax.experimental import pallas as pl
from jax.experimental.pallas import tpu as pltpu
from jax.sharding import PartitionSpec as P


HQ = 32
HK = 4
DH = 128
LOSS_SCALE = 65536
ROWS = 192
CHIP = 2 * ROWS
WIN = 3 * CHIP
GROUP = HQ // HK
SUB = 96
LANES = SUB * GROUP
SPANS = (256, 512, 640, 704, 784, 896)
CHUNKS = 2
TAIL = 16
PACK = CHIP + TAIL
MASKED = -1e30
SCALE = DH ** (-0.5)
LOG2E = 1.4426950408889634
HALVES = 1
PART = LANES // HALVES
SHARED = 384
F32 = jnp.float32
BF16 = jnp.bfloat16


def to_column(row, shift=0):
    n = row.shape[1]
    r = lax.broadcasted_iota(jnp.int32, (n, n), 0)
    c = lax.broadcasted_iota(jnp.int32, (n, n), 1)
    return jnp.sum(jnp.where(c == r + shift, row, 0), axis=1, keepdims=True)


def end_row(starts, seq_len):
    n = starts.shape[1]
    r = lax.broadcasted_iota(jnp.int32, (n, n), 0)
    c = lax.broadcasted_iota(jnp.int32, (n, n), 1)
    col = to_column(starts)
    row = jnp.sum(jnp.where(r == c + 1, col, 0), axis=0, keepdims=True)
    lane = lax.broadcasted_iota(jnp.int32, (1, n), 1)
    return jnp.where(lane == n - 1, seq_len, row)


def pack_kernel(seq_len, idx_ref, kv_ref, got_ref, lr_ref, got_lr_ref, st_ref, ct_ref, *own_refs):
    index = idx_ref[0]
    core = index % 2
    for half in range(2):

        @pl.when(core == half)
        def _():
            for j in range(CHUNKS):
                for k in range(2):
                    lo = k * HK * DH + (half * CHUNKS + j) * DH
                    own_refs[j][0:ROWS, k * DH : (k + 1) * DH] = kv_ref[:, lo : lo + DH]
                    own_refs[j][ROWS:CHIP, k * DH : (k + 1) * DH] = got_ref[:, lo : lo + DH]

    starts = st_ref[...]
    n = starts.shape[1]
    row_i = lax.broadcasted_iota(jnp.int32, (n, 1), 0)
    st = to_column(starts)
    en = jnp.where(row_i == n - 1, seq_len, to_column(starts, 1))
    first = jnp.maximum(st, en - to_column(ct_ref[...]))
    lane = lax.broadcasted_iota(jnp.int32, (n, ROWS), 1)
    part = jnp.zeros((n, 1), F32)
    for ref, where in ((lr_ref, index), (got_lr_ref, index + 1 - 2 * core)):
        pos = where * ROWS + lane
        part = part + jnp.sum(jnp.where((pos >= first) & (pos < en), ref[...], 0.0), axis=1, keepdims=True)
    r = lax.broadcasted_iota(jnp.int32, (n, n), 0)
    c = lax.broadcasted_iota(jnp.int32, (n, n), 1)
    part = jnp.sum(jnp.where(r == c, part, 0.0), axis=0, keepdims=True)
    high = part.astype(BF16).astype(F32)
    rest = part - high
    mid = rest.astype(BF16).astype(F32)
    low = rest - mid
    k = lax.broadcasted_iota(jnp.int32, (TAIL, n), 0)
    tail = jnp.where(k == 0, high, jnp.where(k == 1, mid, jnp.where(k == 2, low, 0.0))).astype(BF16)
    own_refs[0][CHIP:PACK, :] = jnp.zeros((TAIL, 2 * DH), BF16)
    own_refs[0][CHIP:PACK, 0:n] = tail


def early_kernel(kv_hbm, lr_ref, st_ref, ct_ref, kv_ref, lr_out, st_out, ct_out, sem):
    copy = pltpu.make_async_copy(kv_hbm, kv_ref, sem)
    copy.start()
    lr_out[...] = lr_ref[...]
    st_out[...] = st_ref[...]
    ct_out[...] = ct_ref[...]
    copy.wait()


def halves_kernel(idx_ref, q_hbm, g_hbm, snd_ref, q_all, g_all, sems):
    core = idx_ref[0] % 2
    width = q_all.shape[1]
    rows = pl.ds(pl.multiple_of(core * ROWS, ROWS), ROWS)
    mine = pl.ds(pl.multiple_of(core * width, width), width)
    theirs = pl.ds(pl.multiple_of((1 - core) * width, width), width)
    copies = [
        pltpu.make_async_copy(q_hbm.at[:, theirs], snd_ref.at[0], sems.at[0]),
        pltpu.make_async_copy(g_hbm.at[:, theirs], snd_ref.at[1], sems.at[1]),
        pltpu.make_async_copy(q_hbm.at[:, mine], q_all.at[rows], sems.at[2]),
        pltpu.make_async_copy(g_hbm.at[:, mine], g_all.at[rows], sems.at[3]),
    ]
    for copy in copies:
        copy.start()
    for copy in copies:
        copy.wait()


def join_kernel(seq_len, idx_ref, got_ref, q_in, g_in, st_ref, ct_ref, sc_ref, cnt_ref, q_all, g_all):
    core = idx_ref[0] % 2
    mine = pl.ds(pl.multiple_of(core * ROWS, ROWS), ROWS)
    other = pl.ds(pl.multiple_of((1 - core) * ROWS, ROWS), ROWS)
    index = idx_ref[0]
    first = index // 2 * CHIP
    base = first - (WIN - CHIP)
    sc_ref[0] = index % 2
    sc_ref[1] = base
    starts = st_ref[...].astype(F32)
    for s in range(CHIP // SUB):
        at = (first + s * SUB).astype(F32)
        start = jnp.max(jnp.where(starts <= at, starts, 0.0)).astype(jnp.int32)
        low = jnp.maximum(start - base, 0) // 16 * 16
        need = (WIN - CHIP) + (s + 1) * SUB - low
        pick = jnp.int32(0)
        span = jnp.int32(SPANS[0])
        for v in range(1, len(SPANS)):
            more = need > SPANS[v - 1]
            pick = jnp.where(more, v, pick)
            span = jnp.where(more, SPANS[v], span)
        sc_ref[2 + 2 * s] = jnp.minimum(low, WIN - span)
        sc_ref[3 + 2 * s] = pick
    used = jnp.sum(jnp.where(ct_ref[...] > 0, 1.0, 0.0), axis=1, keepdims=True)
    cnt_ref[...] = jnp.broadcast_to(used, cnt_ref.shape)
    slots = st_ref[...]
    ends = end_row(slots, seq_len)
    first_answer = jnp.maximum(slots, ends - ct_ref[...])

    def answers(where):
        pos = where * ROWS + lax.broadcasted_iota(jnp.int32, (ROWS, slots.shape[1]), 0)
        hit = jnp.where((pos >= first_answer) & (pos < ends), 1.0, 0.0)
        return jnp.sum(hit, axis=1, keepdims=True) > 0.5

    q_all[other, :] = got_ref[0]
    g_all[other, :] = jnp.where(answers(index + 1 - 2 * core), got_ref[1], jnp.zeros((), BF16))
    g_all[mine, :] = jnp.where(answers(index), g_in[mine, :], jnp.zeros((), BF16))


def nt(a, b):
    return lax.dot_general(a, b, (((1,), (1,)), ((), ())), preferred_element_type=F32)


def nn(a, b):
    return lax.dot_general(a, b, (((1,), (0,)), ((), ())), preferred_element_type=F32)


def tn(a, b):
    return lax.dot_general(a, b, (((0,), (0,)), ((), ())), preferred_element_type=F32)


def fold(x, op):
    out = x[0:8]
    for i in range(8, x.shape[0], 8):
        out = op(out, x[i : i + 8])
    return out


def attention_kernel(chunk, sc_ref, q_all, g_all, own_ref, a_ref, b_ref, st_ref, *refs):
    refs = refs[1:] if chunk else refs
    dq_own_ref, dq_other_ref, d_own_ref, d_a_ref, d_b_ref, *refs = refs
    k_all, v_all, q_now, g_now, s_buf, d_buf, k_acc, v_acc, dq_now, dq_all = refs
    core = sc_ref[0]
    base = sc_ref[1]
    mine = pl.multiple_of(core * ROWS, ROWS)
    other = pl.multiple_of((1 - core) * ROWS, ROWS)
    width = GROUP * DH
    for i, src in enumerate((b_ref, a_ref, own_ref)):
        for at, lo in ((mine, 0), (other, ROWS)):
            rows = pl.ds(i * CHIP + at, ROWS)
            k_all[rows, :] = src[lo : lo + ROWS, 0:DH]
            v_all[rows, :] = src[lo : lo + ROWS, DH : 2 * DH]
    k_acc[...] = jnp.zeros(k_acc.shape, F32)
    v_acc[...] = jnp.zeros(v_acc.shape, F32)
    starts = st_ref[...]
    st_col = to_column(starts)

    def flush(row_first):
        done = dq_now[...].T
        for h in range(GROUP):
            dq_all[pl.ds(row_first, SUB), h * DH : (h + 1) * DH] = done[h * SUB : (h + 1) * SUB].astype(BF16)

    def span_step(span, key_first, row_first, low, pos):
        pieces = [(o, min(256, span - o)) for o in range(0, span, 256)]
        flush(row_first)
        state = [{} for _ in range(HALVES)]

        def rows_of(o, size):
            return pl.ds(pl.multiple_of(key_first + o, 16), size)

        def score(i, o, size):
            part = slice(i * PART, (i + 1) * PART)
            scores = nt(k_all[rows_of(o, size), :], q_now[part, :])
            key_pos = base + key_first + o + lax.broadcasted_iota(jnp.int32, (size, SHARED), 0)
            seen = (key_pos >= low) & (key_pos <= pos)
            scores = jnp.where(jnp.concatenate([seen] * (PART // SHARED), axis=1), scores, MASKED)
            s_buf[o : o + size, part] = scores
            top = fold(scores, jnp.maximum)
            state[i]["top"] = top if o == 0 else jnp.maximum(state[i]["top"], top)

        def weigh(i, o, size):
            part = slice(i * PART, (i + 1) * PART)
            if o == 0:
                state[i]["peak"] = jnp.max(state[i]["top"], axis=0, keepdims=True) * (SCALE * LOG2E)
            d_probs = nt(v_all[rows_of(o, size), :], g_now[part, :])
            weight = jnp.exp2(s_buf[o : o + size, part] * (SCALE * LOG2E) - state[i]["peak"])
            s_buf[o : o + size, part] = weight
            d_buf[o : o + size, part] = d_probs
            total = fold(weight, jnp.add)
            delta = fold(weight * d_probs, jnp.add)
            state[i]["total"] = total if o == 0 else state[i]["total"] + total
            state[i]["delta"] = delta if o == 0 else state[i]["delta"] + delta

        def finish(i, o, size):
            part = slice(i * PART, (i + 1) * PART)
            if o == 0:
                inverse = 1.0 / jnp.sum(state[i]["total"], axis=0, keepdims=True)
                state[i]["inverse"] = inverse
                state[i]["delta"] = jnp.sum(state[i]["delta"], axis=0, keepdims=True) * inverse
            rows = rows_of(o, size)
            probs = s_buf[o : o + size, part] * state[i]["inverse"]
            d_scores = (probs * (d_buf[o : o + size, part] - state[i]["delta"])).astype(BF16)
            v_acc[rows, :] += nn(probs.astype(BF16), g_now[part, :])
            k_acc[rows, :] += nn(d_scores, q_now[part, :])
            dq = tn(k_all[rows, :], d_scores)
            state[i]["dq"] = dq if o == 0 else state[i]["dq"] + dq

        stages = (score, weigh, finish)
        for t in range(len(stages) + HALVES - 1):
            for o, size in pieces:
                for i in range(HALVES):
                    if 0 <= t - i < len(stages):
                        stages[t - i](i, o, size)
        for i in range(HALVES):
            dq_now[:, i * PART : (i + 1) * PART] = state[i]["dq"] * SCALE

    def step(s, carry):
        key_first = pl.multiple_of(sc_ref[2 + 2 * s], 16)
        pick = sc_ref[3 + 2 * s]
        row_first = pl.multiple_of(s * SUB, SUB)
        for h in range(GROUP):
            col = chunk * width + h * DH
            q_now[h * SUB : (h + 1) * SUB, :] = q_all[pl.ds(row_first, SUB), col : col + DH]
            g_now[h * SUB : (h + 1) * SUB, :] = g_all[pl.ds(row_first, SUB), col : col + DH]
        lane = lax.broadcasted_iota(jnp.int32, (1, SHARED), 1)
        pos = base + (WIN - CHIP) + row_first + lane % SUB
        low = jnp.max(jnp.where(st_col <= pos, st_col, 0), axis=0, keepdims=True)
        for v, span in enumerate(SPANS):
            pl.when(pick == v)(partial(span_step, span, key_first, row_first, low, pos))
        return carry

    lax.fori_loop(0, CHIP // SUB, step, 0)
    flush(CHIP)
    dq_own_ref[...] = dq_all[pl.ds(SUB + mine, ROWS), :]
    dq_other_ref[:, chunk * width : (chunk + 1) * width] = dq_all[pl.ds(SUB + other, ROWS), :]
    for i, dst in enumerate((d_b_ref, d_a_ref, d_own_ref)):
        for at, lo in ((mine, 0), (other, ROWS)):
            rows = pl.ds(i * CHIP + at, ROWS)
            dst[lo : lo + ROWS, 0:DH] = (k_acc[rows, :] * SCALE).astype(dst.dtype)
            dst[lo : lo + ROWS, DH : 2 * DH] = v_acc[rows, :].astype(dst.dtype)
    if chunk == 0:
        d_b_ref[CHIP:PACK, 0:DH] = own_ref[CHIP:PACK, 0:DH]
        d_b_ref[CHIP:PACK, DH : 2 * DH] = a_ref[CHIP:PACK, 0:DH]


def row_coefs(starts, ends, coef, first):
    n = starts.shape[1]
    pos = first + lax.broadcasted_iota(jnp.int32, (ROWS, n), 0)
    return jnp.sum(jnp.where((pos >= starts) & (pos < ends), coef, 0.0), axis=1, keepdims=True)


def query_kernel(idx_ref, scale_ref, *refs):
    mine_refs, got_ref, out_hbm, done, sems = refs[0:2], *refs[2:6]
    scale = scale_ref[:, 0:1]
    width = GROUP * DH
    copies = []
    for k in range(2):
        for j in range(CHUNKS):
            src = got_ref[:, j * width : (j + 1) * width] if k else mine_refs[j][...]
            slot = k * CHUNKS + j
            done[slot] = (src.astype(F32) * scale).astype(BF16)
            at = pl.multiple_of(((idx_ref[0] + k) % 2 * CHUNKS + j) * width, width)
            copies.append(pltpu.make_async_copy(done.at[slot], out_hbm.at[:, pl.ds(at, width)], sems.at[slot]))
            copies[-1].start()
    for copy in copies:
        copy.wait()


def place_kernel(idx_ref, mine_ref, got_ref, out_hbm, sems):
    cut = CHUNKS * DH
    copies = []
    for k, src in enumerate((mine_ref, got_ref)):
        for j in range(2):
            at = pl.multiple_of(j * HK * DH + (idx_ref[0] + k) % 2 * cut, cut)
            copies.append(
                pltpu.make_async_copy(
                    src.at[:, j * cut : (j + 1) * cut], out_hbm.at[:, pl.ds(at, cut)], sems.at[2 * k + j]
                )
            )
            copies[-1].start()
    for copy in copies:
        copy.wait()


def key_value_kernel(seq_len, idx_ref, st_ref, ct_ref, docs_ref, more_ref, *refs):
    tail_refs, own_refs, a_refs, b_refs = refs[0:3], refs[3:5], refs[5:7], refs[7:9]
    outs, scale_ref = refs[9:11], refs[11]
    index = idx_ref[0]
    starts = st_ref[...]
    n = starts.shape[1]
    sums = jnp.zeros((1, n), F32)
    for ref in (*tail_refs, b_refs[0]):
        sums = sums + jnp.sum(ref[CHIP:PACK, 0:n].astype(F32), axis=0, keepdims=True)
    sums = sums + jnp.sum(b_refs[0][CHIP:PACK, DH : DH + n].astype(F32), axis=0, keepdims=True)
    size = jnp.maximum(ct_ref[...], 1).astype(F32)
    docs = docs_ref[0:1, 0:n] + more_ref[0:1, 0:n]
    coef = LOSS_SCALE * 2.0 / (1.0 + jnp.exp(-sums / size)) / (size * docs)
    ends = end_row(starts, seq_len)
    for i, where in enumerate((index, index // 2 * 2 + 1 - index % 2)):
        rows = slice(i * ROWS, (i + 1) * ROWS)
        scale = jnp.broadcast_to(row_coefs(starts, ends, coef, where * ROWS), (ROWS, DH))
        if i == 0:
            scale_ref[...] = scale
        for j in range(CHUNKS):
            for k in range(2):
                cols = slice(k * DH, (k + 1) * DH)
                out = own_refs[j][rows, cols] + a_refs[j][rows, cols].astype(F32) + b_refs[j][rows, cols].astype(F32)
                at = (k * CHUNKS + j) * DH
                outs[i][:, at : at + DH] = (out * scale).astype(BF16)


def in_vmem(x):
    return pltpu.with_memory_space_constraint(x, pltpu.VMEM)


def in_hbm(x):
    return pltpu.with_memory_space_constraint(x, pltpu.HBM)


def local(query, key_value, upstream, log_ratio, doc_starts, answer_counts):
    count = lax.axis_size("ctx")
    seq_len = ROWS * count
    index = lax.axis_index("ctx").astype(jnp.int32)
    where = index.reshape(1)
    smem = pl.BlockSpec(memory_space=pltpu.SMEM)
    vmem = pl.BlockSpec(memory_space=pltpu.VMEM)

    def moved(value, steps):
        return lax.ppermute(value, "ctx", [(i, (i + steps) % count) for i in range(count)])

    def moved_two_chips(value, steps):
        pairs = [(i, i + steps) for i in range(count) if 0 <= i + steps < count]
        senders, receivers = sorted(set(range(count)) - {i for i, _ in pairs}), sorted(set(range(count)) - {i for _, i in pairs})
        half = len(senders) // 2
        return lax.ppermute(value, "ctx", pairs + list(zip(senders, receivers[half:] + receivers[:half])))

    def swapped(value):
        return lax.ppermute(value, "ctx", [(i, i ^ 1) for i in range(count)])

    def exchanged(value, bit):
        return lax.ppermute(value, "dp", [(i, i ^ bit) for i in range(lax.axis_size("dp"))])

    width = GROUP * DH
    got_lr = swapped(log_ratio)
    got_kv = swapped(key_value[0])
    hbm = pl.BlockSpec(memory_space=pl.ANY)
    slots = doc_starts.shape[1]
    own_kv, ratios, starts, counts = pl.pallas_call(
        early_kernel,
        out_shape=(
            pltpu.VMEM((ROWS, 2 * HK * DH), BF16),
            pltpu.VMEM((1, ROWS), F32),
            pltpu.VMEM((1, slots), jnp.int32),
            pltpu.VMEM((1, slots), jnp.int32),
        ),
        in_specs=[hbm] + [vmem] * 3,
        out_specs=(vmem,) * 4,
        scratch_shapes=[pltpu.SemaphoreType.DMA],
        compiler_params=pltpu.CompilerParams(vmem_limit_bytes=4 << 20),
        name="early",
    )(*[in_hbm(x) for x in (key_value[0], log_ratio, doc_starts, answer_counts)])
    packed = [pltpu.VMEM((CHIP if j else PACK, 2 * DH), BF16) for j in range(CHUNKS)]
    own = pl.pallas_call(
        partial(pack_kernel, seq_len),
        out_shape=tuple(packed),
        in_specs=[smem] + [vmem] * 6,
        out_specs=(vmem,) * CHUNKS,
        compiler_params=pltpu.CompilerParams(vmem_limit_bytes=4 << 20),
        name="pack",
    )(where, *[in_vmem(x) for x in (own_kv, got_kv, ratios, got_lr, starts, counts)])
    back1, back2 = [], []
    for j in range(CHUNKS):
        back1.append(moved(own[j], 2))
        back2.append(moved_two_chips(own[j], 4))
    joint = pltpu.VMEM((CHIP, CHUNKS * width), BF16)
    to_send, q_mine, g_mine = pl.pallas_call(
        halves_kernel,
        out_shape=(pltpu.VMEM((2, ROWS, CHUNKS * width), BF16), joint, joint),
        in_specs=[smem, hbm, hbm],
        out_specs=(vmem,) * 3,
        scratch_shapes=[pltpu.SemaphoreType.DMA((4,))],
        compiler_params=pltpu.CompilerParams(vmem_limit_bytes=8 << 20),
        name="halves",
    )(where, in_hbm(query[0]), in_hbm(upstream[0]))
    got_rows = swapped(to_send)
    scalars, docs, q_all, g_all = pl.pallas_call(
        partial(join_kernel, seq_len),
        out_shape=(
            jax.ShapeDtypeStruct((2 + 2 * (CHIP // SUB),), jnp.int32),
            pltpu.VMEM((8, 128), F32),
            joint,
            joint,
        ),
        in_specs=[smem] + [vmem] * 5,
        out_specs=(smem,) + (vmem,) * 3,
        input_output_aliases={2: 2, 3: 3},
        compiler_params=pltpu.CompilerParams(vmem_limit_bytes=8 << 20),
        name="join",
    )(where, *[in_vmem(x) for x in (got_rows, q_mine, g_mine, starts, counts)])
    more_docs = exchanged(docs, 1)

    dq_mine, dq_other, d_own, d_a, d_b = [], [], [], [], []
    for j in range(CHUNKS):
        operands = (q_all, g_all, own[j], back1[j], back2[j], starts, *dq_other[-1:])
        outs = pl.pallas_call(
            partial(attention_kernel, j),
            in_specs=[smem] + [vmem] * len(operands),
            input_output_aliases={len(operands): 1} if j else {},
            out_specs=[vmem] * 5,
            scratch_shapes=[
                pltpu.VMEM((WIN, DH), BF16),
                pltpu.VMEM((WIN, DH), BF16),
                pltpu.VMEM((LANES, DH), BF16),
                pltpu.VMEM((LANES, DH), BF16),
                pltpu.VMEM((SPANS[-1], LANES), F32),
                pltpu.VMEM((SPANS[-1], LANES), F32),
                pltpu.VMEM((WIN, DH), F32),
                pltpu.VMEM((WIN, DH), F32),
                pltpu.VMEM((DH, LANES), F32),
                pltpu.VMEM((SUB + CHIP, width), BF16),
            ],
            out_shape=[
                pltpu.VMEM((ROWS, width), BF16),
                pltpu.VMEM((ROWS, CHUNKS * width), BF16),
                pltpu.VMEM((CHIP, 2 * DH), F32),
                pltpu.VMEM((CHIP, 2 * DH), BF16),
                packed[j],
            ],
            compiler_params=pltpu.CompilerParams(vmem_limit_bytes=24 << 20),
        )(scalars, *[in_vmem(x) for x in operands])
        for kept, out in zip((dq_mine, dq_other, d_own, d_a, d_b), outs):
            kept.append(out)

    got_a, got_b = [], []
    for j in range(CHUNKS):
        got_a.append(moved(d_a[j], -2))
        got_b.append((moved_two_chips if j else moved)(d_b[j], -4))
    dq_got = swapped(dq_other[-1])
    docs = docs + more_docs
    more_docs = exchanged(docs, 2)
    half = pltpu.VMEM((ROWS, 2 * CHUNKS * DH), BF16)
    operands = (starts, counts, docs, more_docs, own[0], back1[0], back2[0], *d_own, *got_a, *got_b)
    kv_mine, kv_send, scale = pl.pallas_call(
        partial(key_value_kernel, seq_len),
        out_shape=(half, half, pltpu.VMEM((ROWS, DH), F32)),
        in_specs=[smem] + [vmem] * len(operands),
        out_specs=(vmem,) * 3,
        compiler_params=pltpu.CompilerParams(vmem_limit_bytes=8 << 20),
        name="kv_out",
    )(where, *[in_vmem(x) for x in operands])
    kv_got = swapped(kv_send)
    d_query = pl.pallas_call(
        query_kernel,
        out_shape=jax.ShapeDtypeStruct((ROWS, HQ * DH), BF16),
        in_specs=[smem] + [vmem] * 4,
        out_specs=hbm,
        scratch_shapes=[pltpu.VMEM((2 * CHUNKS, ROWS, width), BF16), pltpu.SemaphoreType.DMA((2 * CHUNKS,))],
        compiler_params=pltpu.CompilerParams(vmem_limit_bytes=8 << 20),
        name="q_out",
    )(where, *[in_vmem(x) for x in (scale, *dq_mine, dq_got)])
    d_key_value = pl.pallas_call(
        place_kernel,
        out_shape=jax.ShapeDtypeStruct((ROWS, 2 * HK * DH), BF16),
        in_specs=[smem, vmem, vmem],
        out_specs=hbm,
        scratch_shapes=[pltpu.SemaphoreType.DMA((4,))],
        name="place",
    )(where, in_vmem(kv_mine), in_vmem(kv_got))
    return (d_query[None], d_key_value[None])


def solution(mesh):
    return jax.shard_map(
        local,
        mesh=mesh,
        in_specs=(
            P("dp", "ctx", None),
            P("dp", "ctx", None),
            P("dp", "ctx", None),
            P("dp", "ctx"),
            P("dp", None),
            P("dp", None),
        ),
        out_specs=(P("dp", "ctx", None), P("dp", "ctx", None)),
        check_vma=False,
    )
```
